256 devices in a mesh: segment: 4 (over x), expert: 32 (over z, y), dp: 2 (over core).
Axes of the slice: x: 4, y: 4, z: 8, core: 2. Of those that a mesh axis runs over, the one named last changes fastest.
Arguments:
- entering: bfloat16 [4, 4096, 2560], P('segment', ('expert', 'dp')), may hold values from -0.59765625 to 0.59765625
- fresh: bfloat16 [1, 4096, 2560], P(None, ('expert', 'dp')), may hold values from -0.59765625 to 0.59765625
- w_gate: bfloat16 [4, 64, 2560, 768], P('segment', ('expert', 'dp')), may hold values from -0.125 to 0.125
- w_up: bfloat16 [4, 64, 2560, 768], P('segment', ('expert', 'dp')), may hold values from -0.125 to 0.125
- w_down: bfloat16 [4, 64, 768, 2560], P('segment', ('expert', 'dp')), may hold values from -0.21875 to 0.21875
- router: bfloat16 [4, 2560, 64], P('segment'), may hold values from -0.0625 to 0.0625
- gain: float32 [4, 2560], P('segment'), may hold values from 0.5 to 2
- routes: int32 [4, 2, 4096, 6], P('segment', None, ('expert', 'dp')), may hold values from 0 to 63, all different within a row; in each aligned block of 64 rows (0 to 63, 64 to 127, ..., all dimensions but the last counted through in order) at most 8 rows name the same one
Outputs:
- section_out: bfloat16 [4, 2, 4096, 2560], P('segment', None, ('expert', 'dp'))
The draws below stay inside these ranges and needn't reach their ends.
Inputs may be any that keep to these rules, and one draw needn't show every extreme that they name: `routes`: in every aligned block of 64 rows (the tokens of one device for one section and micro-batch) no expert is named by more than 8 rows, and in some blocks one expert is named by exactly 8 rows; a row names 6 different experts.
All inputs are finite; a program needn't handle non-finite values.
Results may differ from the reference program's by a relative error of at most 0.009.
Values may be sent and summed in bfloat16 or wider, within the bound.
No kernel may reach another device: no remote copies, remote signals or barrier semaphores. Data moves between devices by JAX's collectives and lax.ppermute only.
A program may use at most 64 MiB of HBM per device.

```python
import math
import jax
import jax.numpy as jnp
import numpy as np
from jax import lax

D = 2560
HID = 768
TOPK = 6
MICRO = 2
TOK_DEV = 64
LAYERS = 4
EXPERTS = 64
TOKENS = 4096
CAP = 8


def block_scale(key, dims, split, low, largest):
    level, own = 1.0, jax.random.fold_in(key, 6)
    for position, shards_of in split:
        steps = jnp.exp(jax.random.uniform(jax.random.fold_in(own, position), (shards_of,), jnp.float32, low / len(split), largest / len(split)))
        level = level * jnp.repeat(steps, dims[position] // shards_of).reshape([-1 if axis == position else 1 for axis in range(len(dims))])
    return level


def deal_out(stream_key, own, number, rows, number_of, top, bound, slope):
    sequence = jax.random.permutation(stream_key, number_of)
    heavy_load, common = load_shares(number_of, rows * top, bound, slope, True), load_shares(number_of, rows * top, bound, slope, False)
    places = jnp.arange(number_of)

    def named(tallies, turn):
        used = int((tallies > 0).sum())
        fixed = max(1, used // 4)
        shifted = fixed + (places - fixed + turn * (used - fixed)) % max(1, number_of - fixed)
        return jnp.zeros((number_of,), jnp.int32).at[sequence[jnp.where(places < fixed, places, shifted)]].set(jnp.asarray(tallies, jnp.int32))

    tallies = jnp.where(number % 4 == 0, named(heavy_load, number // 4), named(common, number - number // 4 - 1))
    mixed = jax.random.permutation(jax.random.fold_in(own, 3), number_of)
    giver, receiver = mixed[0:number_of // 2 * 2:2], mixed[1:number_of // 2 * 2:2]
    margin = jnp.minimum(tallies[giver] - 1, bound - tallies[receiver]) // 2
    margin = jnp.where((giver == sequence[0]) | (receiver == sequence[0]) | (tallies[receiver] == 0), 0, jnp.maximum(margin, 0))
    shifted = jax.random.randint(jax.random.fold_in(own, 4), (number_of // 2,), 0, 1 << 20) % (margin + 1)
    tallies = tallies.at[giver].add(-shifted).at[receiver].add(shifted)
    labels = jnp.searchsorted(jnp.cumsum(tallies), jnp.arange(rows * top), side="right").astype(jnp.int32)
    grid = labels.reshape(top, rows).T
    grid = grid[jax.random.permutation(jax.random.fold_in(own, 1), rows)]
    turn = jax.random.randint(jax.random.fold_in(own, 2), (rows, 1), 0, top)
    return jnp.take_along_axis(grid, (jnp.arange(top)[None, :] + turn) % top, axis=1)


def load_shares(amount, total, limit, lean, full):
    portions = [(1 << 20) // math.isqrt(rank ** lean) + 1 for rank in range(1, amount + 1)]
    largest = limit if full else min(limit, max(-(-total // amount), total * portions[0] // sum(portions)))
    least = 1 if total - largest >= amount - 1 else 0
    given, spare = [largest] + [least] * (amount - 1), total - largest - least * (amount - 1)
    while spare > 0:
        movable = [i for i in range(1, amount) if given[i] < largest] or [i for i in range(1, amount) if given[i] < limit]
        mass, remaining = sum([portions[i] for i in movable]), spare
        for i in movable:
            extra = min(limit - given[i], max(1, remaining * portions[i] // mass), spare)
            given[i] = given[i] + extra
            spare = spare - extra
    return np.array(given)


def bell_draw(stream_key, shape, spread, reach, shards=(), held_as=jnp.bfloat16):
    factor_of = block_scale(stream_key, shape, shards, -0.22, 0.18) if shards else 1.0
    drawn = jax.random.normal(stream_key, shape, jnp.float32) * spread * factor_of
    return jnp.minimum(jnp.maximum(drawn, -reach), reach).astype(held_as)


def setup_inputs(seed: int = 0) -> dict:
    streams_of = jax.random.split(jax.random.key(seed), 9)
    entering = bell_draw(streams_of[0], (LAYERS, TOKENS, D), 0.1, 0.59765625, ((0, 4), (1, 64)))
    fresh = bell_draw(streams_of[1], (MICRO - 1, TOKENS, D), 0.1, 0.59765625, ((1, 64),))
    w_gate = bell_draw(streams_of[2], (LAYERS, EXPERTS, D, HID), D ** -0.5, 0.125, ((0, 4), (1, 64)))
    w_up = bell_draw(streams_of[3], (LAYERS, EXPERTS, D, HID), D ** -0.5, 0.125, ((0, 4), (1, 64)))
    w_down = bell_draw(streams_of[4], (LAYERS, EXPERTS, HID, D), HID ** -0.5, 0.21875, ((0, 4), (1, 64)))
    router = bell_draw(streams_of[5], (LAYERS, D, EXPERTS), (4 * D) ** -0.5, 0.0625, ((0, 4),))
    gain = jnp.clip(jnp.exp(math.log(2.0) - 1.3862944 * jax.random.uniform(streams_of[6], (LAYERS, D), jnp.float32) ** block_scale(streams_of[6], (LAYERS, D), ((0, 4),), -0.2, 0.2)), 0.5, 2.0)
    routes_keys = jax.random.split(jax.random.fold_in(streams_of[7], 1), LAYERS * MICRO * TOKENS // TOK_DEV)
    routes_turns = jax.random.permutation(jax.random.fold_in(streams_of[7], 3), LAYERS * MICRO * TOKENS // TOK_DEV)
    routes = jax.vmap(lambda own, number: deal_out(jax.random.fold_in(streams_of[7], 2), own, number, TOK_DEV, EXPERTS, TOPK, CAP, 2))(routes_keys, routes_turns).reshape((LAYERS, MICRO, TOKENS, TOPK))
    return dict(entering=entering, fresh=fresh, w_gate=w_gate, w_up=w_up, w_down=w_down, router=router, gain=gain, routes=routes)


def expert_rows(slot_rows, gate_weight, up_weight, down_weight):
    model_width = slot_rows.shape[-1]
    flattened = slot_rows.reshape(-1, model_width)
    gate_out = jnp.dot(flattened, gate_weight, preferred_element_type=jnp.float32)
    upper = jnp.dot(flattened, up_weight, preferred_element_type=jnp.float32)
    hidden = (jax.nn.silu(gate_out) * upper).astype(jnp.bfloat16)
    projected = jnp.dot(hidden, down_weight, preferred_element_type=jnp.float32).astype(jnp.bfloat16)
    return projected.reshape(slot_rows.shape)

def routed_slots(chosen_ids, expert_count):
    onehot = (chosen_ids[:, None] == jnp.arange(expert_count, dtype=jnp.int32)[None, :]).astype(jnp.int32)
    before = jnp.cumsum(onehot, axis=0) - onehot
    return lax.optimization_barrier(jnp.sum(before * onehot, axis=1)).astype(jnp.int32)

def section_all(incoming, gate_weight, up_weight, down_weight, router_layer, gain_layer, chosen_ids):
    device_count = TOKENS // TOK_DEV
    values = incoming.astype(jnp.float32)
    inv_scale = lax.rsqrt(lax.optimization_barrier(jnp.mean(values * values, axis=1, keepdims=True)) + 1e-06)
    normed = (values * inv_scale * gain_layer[None, :]).astype(jnp.bfloat16)
    logits = jnp.dot(normed, router_layer, preferred_element_type=jnp.float32)
    scores = jax.nn.sigmoid(logits)
    chosen = jnp.take_along_axis(scores, chosen_ids, axis=1)
    mixing = chosen / lax.optimization_barrier(jnp.sum(chosen, axis=1, keepdims=True))
    block_ids = chosen_ids.reshape(device_count, TOK_DEV * TOPK).astype(jnp.int32)
    slot_ids = jax.vmap(lambda ids: routed_slots(ids, EXPERTS))(block_ids)
    owners = jnp.broadcast_to((jnp.arange(TOK_DEV * TOPK, dtype=jnp.int32) // TOPK)[None, :], block_ids.shape)
    device_ids = jnp.broadcast_to(jnp.arange(device_count, dtype=jnp.int32)[:, None], block_ids.shape)
    source = jnp.full((device_count, EXPERTS, CAP), TOK_DEV, jnp.int32).at[device_ids, block_ids, slot_ids].set(owners)
    padded = jnp.concatenate([normed.reshape(device_count, TOK_DEV, D), jnp.zeros((device_count, 1, D), jnp.bfloat16)], axis=1)
    outgoing = jax.vmap(lambda table, where_from: table[where_from])(padded, source)
    arranged = jnp.swapaxes(outgoing, 0, 1)
    processed = lax.map(lambda packed: expert_rows(packed[0], packed[1], packed[2], packed[3]), (arranged, gate_weight, up_weight, down_weight))
    landed = processed[block_ids, device_ids, slot_ids].reshape(TOKENS, TOPK, D)
    summed = values + lax.optimization_barrier(jnp.sum(landed.astype(jnp.float32) * mixing[:, :, None], axis=1))
    return summed.astype(jnp.bfloat16)

def reference(entering, fresh, w_gate, w_up, w_down, router, gain, routes):
    outputs_all = []
    previous = None
    for step_index in range(MICRO):
        row_list = []
        for segment_index in range(LAYERS):
            if step_index == 0:
                incoming = entering[segment_index]
            elif segment_index == 0:
                incoming = fresh[step_index - 1]
            else:
                incoming = previous[segment_index - 1]
            row_list.append(section_all(incoming, w_gate[segment_index], w_up[segment_index], w_down[segment_index], router[segment_index], gain[segment_index], routes[segment_index, step_index]))
        previous = row_list
        outputs_all.append(row_list)
    return jnp.stack([jnp.stack([outputs_all[step_index][segment_index] for step_index in range(MICRO)]) for segment_index in range(LAYERS)])
```

```python
import jax
import jax.numpy as jnp
from jax import lax
from jax.experimental import pallas as pl
from jax.experimental.pallas import tpu as pltpu
from jax.sharding import PartitionSpec as P

CAP = 8
GROUP = ("expert", "dp")


def dot(lhs, rhs, lhs_dim=1, rhs_dim=0):
    return lax.dot_general(
        lhs, rhs, (((lhs_dim,), (rhs_dim,)), ((), ())), preferred_element_type=jnp.float32
    )


def column_tiles(width, tile):
    return [slice(start, min(start + tile, width)) for start in range(0, width, tile)]


def prepare_kernel(first_ref, arrived_ref, fresh_ref, gain_ref, router_ref, picks_ref,
                   current_ref, rows_ref, weights_ref):
    tokens, width = current_ref.shape
    experts = router_ref.shape[0]
    picked = arrived_ref[...]
    current = jnp.where(first_ref[0] == 1, fresh_ref[...], picked)
    current_ref[...] = current
    values = current.astype(jnp.float32)
    inv_scale = lax.rsqrt(jnp.mean(values * values, axis=1, keepdims=True) + 1e-06)
    normed = (values * inv_scale * gain_ref[...]).astype(jnp.bfloat16)
    logits = dot(router_ref[...], normed, 1, 1)
    expert_ids = lax.broadcasted_iota(jnp.int32, (experts, tokens), 0)
    chosen = jnp.zeros((experts, tokens), jnp.float32)
    for choice in range(picks_ref.shape[0]):
        chosen = chosen + jnp.where(picks_ref[choice : choice + 1, :] == expert_ids, 1.0, 0.0)
    scores = chosen / (1.0 + jnp.exp(-logits))
    mixing = scores / jnp.sum(scores, axis=0, keepdims=True)
    before = jnp.where(
        lax.broadcasted_iota(jnp.int32, (tokens, tokens), 0)
        < lax.broadcasted_iota(jnp.int32, (tokens, tokens), 1), 1.0, 0.0
    ).astype(jnp.bfloat16)
    rank = dot(chosen.astype(jnp.bfloat16), before)
    slot = jnp.where(chosen > 0.0, rank, float(CAP))
    slot_rows = jnp.broadcast_to(slot[:, None, :], (experts, CAP, tokens))
    slot_ids = lax.broadcasted_iota(jnp.int32, (experts, CAP, tokens), 1).astype(jnp.float32)
    here = slot_rows == slot_ids
    pick = jnp.where(here, 1.0, 0.0).reshape(experts * CAP, tokens).astype(jnp.bfloat16)
    mixed = jnp.where(here, jnp.broadcast_to(mixing[:, None, :], here.shape), 0.0)
    weights_ref[...] = mixed.reshape(experts * CAP, tokens).astype(jnp.bfloat16)
    for cols in column_tiles(width, 512):
        rows_ref[:, cols] = dot(pick, normed[:, cols]).astype(jnp.bfloat16)


def prepare(first, arrived, fresh, gain, router, picks):
    tokens, width = arrived.shape
    slots = router.shape[0] * CAP
    vmem = pl.BlockSpec(memory_space=pltpu.VMEM)
    return pl.pallas_call(
        prepare_kernel,
        out_shape=(
            jax.ShapeDtypeStruct((tokens, width), jnp.bfloat16),
            jax.ShapeDtypeStruct((slots, width), jnp.bfloat16),
            jax.ShapeDtypeStruct((slots, tokens), jnp.bfloat16),
        ),
        in_specs=[pl.BlockSpec(memory_space=pltpu.SMEM)] + [vmem] * 5,
        out_specs=(vmem, vmem, vmem),
        name="prepare",
    )(first, arrived, fresh, gain, router, picks)


def experts_kernel(rows_ref, gate_ref, up_ref, down_ref, out_ref, total_ref):
    step = pl.program_id(0)
    rows = rows_ref[...]
    gate = dot(rows, gate_ref[...])
    up = dot(rows, up_ref[...])
    hidden = (gate / (1.0 + jnp.exp(-gate)) * up).astype(jnp.bfloat16)
    width = out_ref.shape[1]
    steps = pl.num_programs(0)

    @pl.when(step == 0)
    def _():
        for cols in column_tiles(width, 512):
            total_ref[:, cols] = dot(hidden, down_ref[:, cols])

    @pl.when((step > 0) & (step < steps - 1))
    def _():
        for cols in column_tiles(width, 512):
            total_ref[:, cols] += dot(hidden, down_ref[:, cols])

    @pl.when(step == steps - 1)
    def _():
        for cols in column_tiles(width, 512):
            out_ref[:, cols] = (total_ref[:, cols] + dot(hidden, down_ref[:, cols])).astype(jnp.bfloat16)


def run_experts(rows, w_gate, w_up, w_down):
    count, width = rows.shape
    hidden = w_gate.shape[1]
    tile = 256
    return pl.pallas_call(
        experts_kernel,
        out_shape=jax.ShapeDtypeStruct((count, width), jnp.bfloat16),
        grid_spec=pltpu.PrefetchScalarGridSpec(
            num_scalar_prefetch=0,
            grid=(hidden // tile,),
            in_specs=[
                pl.BlockSpec((count, width), lambda i: (0, 0)),
                pl.BlockSpec((width, tile), lambda i: (0, i)),
                pl.BlockSpec((width, tile), lambda i: (0, i)),
                pl.BlockSpec((tile, width), lambda i: (i, 0)),
            ],
            out_specs=pl.BlockSpec((count, width), lambda i: (0, 0)),
            scratch_shapes=[pltpu.VMEM((count, width), jnp.float32)],
        ),
        compiler_params=pltpu.CompilerParams(vmem_limit_bytes=40 << 20),
        name="experts",
    )(rows, w_gate, w_up, w_down)


def combine_kernel(current_ref, weights_ref, landed_ref, out_ref):
    weights = jnp.transpose(weights_ref[...])
    for cols in column_tiles(out_ref.shape[1], 512):
        total = current_ref[:, cols].astype(jnp.float32) + dot(weights, landed_ref[:, cols])
        out_ref[:, cols] = total.astype(jnp.bfloat16)


def combine(current, weights, landed):
    vmem = pl.BlockSpec(memory_space=pltpu.VMEM)
    return pl.pallas_call(
        combine_kernel,
        out_shape=jax.ShapeDtypeStruct(current.shape, jnp.bfloat16),
        in_specs=[vmem] * 3,
        out_specs=vmem,
        name="combine",
    )(current, weights, landed)


def exchange(rows):
    count, width = rows.shape
    parts = rows.reshape(count // CAP, CAP, width)
    moved = lax.all_to_all(parts, GROUP, split_axis=0, concat_axis=0, tiled=True)
    return moved.reshape(count, width)


def shards(entering, fresh, w_gate, w_up, w_down, router, gain, routes):
    at_start = (lax.axis_index("segment") == 0).astype(jnp.int32).reshape(1)
    never = jnp.zeros((1,), jnp.int32)
    router_rows = jnp.transpose(router[0])
    picks = jnp.transpose(routes[0], (0, 2, 1))
    results = []
    count = lax.axis_size("segment")
    for step in range(routes.shape[1]):
        if step == 0:
            first, arrived, other = never, entering[0], entering[0]
        else:
            arrived = lax.ppermute(results[-1], "segment", [(i, i + 1) for i in range(count - 1)])
            first, other = at_start, fresh[step - 1]
        current, rows, weights = prepare(first, arrived, other, gain, router_rows, picks[step])
        outputs = run_experts(exchange(rows), w_gate[0, 0], w_up[0, 0], w_down[0, 0])
        results.append(combine(current, weights, exchange(outputs)))
    return jnp.stack(results)[None]


def solution(mesh):
    tokens = P("segment", ("expert", "dp"), None)
    weights = P("segment", ("expert", "dp"), None, None)
    in_specs = (
        tokens, P(None, ("expert", "dp"), None), weights, weights, weights,
        P("segment", None, None), P("segment", None), P("segment", None, ("expert", "dp"), None),
    )
    out_specs = P("segment", None, ("expert", "dp"), None)
    return jax.shard_map(shards, mesh=mesh, in_specs=in_specs, out_specs=out_specs, check_vma=False)
```

```python
import jax
import jax.numpy as jnp
from jax import lax
from jax.experimental import pallas as pl
from jax.experimental.pallas import tpu as pltpu
from jax.sharding import PartitionSpec as P

CAP = 8
LANES = 128
GROUP = ("expert", "dp")
Z, Y, C = 8, 4, 2
VMEM = pl.BlockSpec(memory_space=pltpu.VMEM)
SMEM = pl.BlockSpec(memory_space=pltpu.SMEM)


def dot(lhs, rhs, lhs_dim=1, rhs_dim=0):
    return lax.dot_general(
        lhs, rhs, (((lhs_dim,), (rhs_dim,)), ((), ())), preferred_element_type=jnp.float32
    )


def column_tiles(width, tile):
    return [slice(start, min(start + tile, width)) for start in range(0, width, tile)]


def iota(shape, dim):
    return lax.broadcasted_iota(jnp.int32, shape, dim)


def move(value, target):
    pairs = []
    for z in range(Z):
        for y in range(Y):
            for core in range(C):
                to_z, to_y, to_core = target(z, y, core)
                pairs.append(((z * Y + y) * C + core, ((to_z % Z) * Y + to_y % Y) * C + to_core))
    return lax.ppermute(value, GROUP, pairs)


def to_other_core(value):
    return move(value, lambda z, y, core: (z, y, 1 - core))


def along_y(value, steps):
    return value if steps == 0 else move(value, lambda z, y, core: (z, y + steps, core))


def outward(value):
    return move(value, lambda z, y, core: (z + 1 - 2 * core, y, core))


def homeward(value):
    return move(value, lambda z, y, core: (z - 1 + 2 * core, y, core))


def prepare_kernel(first_ref, arrived_ref, fresh_ref, gain_ref, router_ref, picks_ref,
                   current_ref, packed_ref):
    tokens, width = current_ref.shape
    experts = router_ref.shape[0]
    current = jnp.where(first_ref[0] == 1, fresh_ref[...], arrived_ref[...])
    current_ref[...] = current
    values = current.astype(jnp.float32)
    inv_scale = lax.rsqrt(jnp.mean(values * values, axis=1, keepdims=True) + 1e-06)
    normed = (values * inv_scale * gain_ref[...]).astype(jnp.bfloat16)
    packed_ref[:, :width] = normed
    logits = dot(normed, router_ref[...], 1, 1)
    expert_ids = iota((experts, tokens), 0)
    chosen_rows = jnp.zeros((experts, tokens), jnp.float32)
    for choice in range(picks_ref.shape[0]):
        chosen_rows += jnp.where(picks_ref[choice : choice + 1, :] == expert_ids, 1.0, 0.0)
    chosen_rows = chosen_rows.astype(jnp.bfloat16)
    row, column = iota((tokens, tokens), 0), iota((tokens, tokens), 1)
    chosen = dot(jnp.where(row == column, 1.0, 0.0).astype(jnp.bfloat16), chosen_rows, 1, 1)
    rank = dot(jnp.where(column < row, 1.0, 0.0).astype(jnp.bfloat16), chosen_rows, 1, 1)
    scores = chosen / (1.0 + jnp.exp(-logits))
    mixing = scores / jnp.sum(scores, axis=1, keepdims=True)
    slot = jnp.where(chosen > 0.0, rank, float(CAP))
    packed_ref[:, width:] = jnp.concatenate([slot, mixing], axis=1).astype(jnp.bfloat16)


def prepare(first, arrived, fresh, gain, router, picks):
    tokens, width = arrived.shape
    return pl.pallas_call(
        prepare_kernel,
        out_shape=(
            jax.ShapeDtypeStruct((tokens, width), jnp.bfloat16),
            jax.ShapeDtypeStruct((tokens, width + LANES), jnp.bfloat16),
        ),
        in_specs=[SMEM] + [VMEM] * 5,
        out_specs=(VMEM, VMEM),
        name="prepare",
    )(first, arrived, fresh, gain, router, picks)


def dispatch_kernel(block, count, ids_ref, *refs):
    packed_refs, row_refs, weights_ref = refs[:count], refs[count : count + Y], refs[count + Y]
    width = row_refs[0].shape[1]
    rows = row_refs[0].shape[0]
    notes = jnp.concatenate([ref[:, width:] for ref in packed_refs], axis=0)
    tokens = notes.shape[0]
    line, lane = iota((16, LANES), 0), iota((16, LANES), 1)
    select = jnp.zeros((16, LANES), jnp.float32)
    for step in range(Y):
        hit = (line == step) & (lane == ids_ref[step])
        hit |= (line == step + 8) & (lane == ids_ref[step] + LANES // 2)
        select = jnp.where(hit, 1.0, select)
    picked = dot(select.astype(jnp.bfloat16), notes, 1, 1)
    row, token = iota((rows, tokens), 0), iota((rows, tokens), 1)
    code = jnp.where(token // block == row // CAP, row % CAP, -1).astype(jnp.float32)
    picks = []
    for step in range(Y):
        here = jnp.broadcast_to(picked[step : step + 1, :], (rows, tokens)) == code
        mixing = jnp.broadcast_to(picked[step + 8 : step + 9, :], (rows, tokens))
        picks.append(jnp.where(here, 1.0, 0.0))
        weights_ref[step * rows : (step + 1) * rows, :] = jnp.where(here, mixing, 0.0).astype(jnp.bfloat16)
    pick = jnp.concatenate(picks, axis=0).astype(jnp.bfloat16)
    for cols in column_tiles(width, 512):
        values = jnp.concatenate([ref[:, cols] for ref in packed_refs], axis=0)
        result = dot(pick, values).astype(jnp.bfloat16)
        for step in range(Y):
            row_refs[step][:, cols] = result[step * rows : (step + 1) * rows]


def dispatch(ids, packed, block):
    width = packed[0].shape[1] - LANES
    tokens = sum(value.shape[0] for value in packed)
    rows = tokens // block * CAP
    result = pl.pallas_call(
        lambda *refs: dispatch_kernel(block, len(packed), *refs),
        out_shape=[jax.ShapeDtypeStruct((rows, width), jnp.bfloat16)] * Y
        + [jax.ShapeDtypeStruct((Y * rows, tokens), jnp.bfloat16)],
        in_specs=[SMEM] + [VMEM] * len(packed),
        out_specs=[VMEM] * (Y + 1),
        name="dispatch",
    )(ids, *packed)
    return result[:Y], result[Y]


def experts_kernel(count, *refs):
    row_refs, gate_ref, up_ref, down_ref = refs[:count], refs[count], refs[count + 1], refs[count + 2]
    out_refs, held_ref, total_ref = refs[count + 3 : 2 * count + 3], refs[2 * count + 3], refs[2 * count + 4]
    step, steps = pl.program_id(0), pl.num_programs(0)
    width = total_ref.shape[1]
    starts = [0]
    for ref in row_refs:
        starts.append(starts[-1] + ref.shape[0])

    @pl.when(step == 0)
    def _():
        for index, ref in enumerate(row_refs):
            held_ref[starts[index] : starts[index + 1], :] = ref[...]

    rows = held_ref[...]
    gate = dot(rows, gate_ref[...])
    up = dot(rows, up_ref[...])
    hidden = (gate / (1.0 + jnp.exp(-gate)) * up).astype(jnp.bfloat16)

    @pl.when(step == 0)
    def _():
        for cols in column_tiles(width, 512):
            total_ref[:, cols] = dot(hidden, down_ref[:, cols])

    @pl.when((step > 0) & (step < steps - 1))
    def _():
        for cols in column_tiles(width, 512):
            total_ref[:, cols] += dot(hidden, down_ref[:, cols])

    @pl.when(step == steps - 1)
    def _():
        for cols in column_tiles(width, 512):
            result = (total_ref[:, cols] + dot(hidden, down_ref[:, cols])).astype(jnp.bfloat16)
            for index, ref in enumerate(out_refs):
                ref[:, cols] = result[starts[index] : starts[index + 1]]


def run_experts(row_arrays, w_gate, w_up, w_down):
    width, hidden = w_gate.shape
    count = sum(value.shape[0] for value in row_arrays)
    tile = 256
    whole = [pl.BlockSpec(value.shape, lambda i: (0, 0)) for value in row_arrays]
    return pl.pallas_call(
        lambda *refs: experts_kernel(len(row_arrays), *refs),
        out_shape=[jax.ShapeDtypeStruct(value.shape, jnp.bfloat16) for value in row_arrays],
        grid_spec=pltpu.PrefetchScalarGridSpec(
            num_scalar_prefetch=0,
            grid=(hidden // tile,),
            in_specs=whole
            + [
                pl.BlockSpec((width, tile), lambda i: (0, i)),
                pl.BlockSpec((width, tile), lambda i: (0, i)),
                pl.BlockSpec((tile, width), lambda i: (i, 0)),
            ],
            out_specs=whole,
            scratch_shapes=[pltpu.VMEM((count, width), jnp.bfloat16), pltpu.VMEM((count, width), jnp.float32)],
        ),
        compiler_params=pltpu.CompilerParams(vmem_limit_bytes=40 << 20),
        name="experts",
    )(*row_arrays, w_gate, w_up, w_down)


def combine_kernel(weights_ref, *refs):
    landed_refs, out_refs = refs[:Y], refs[Y:]
    weights = jnp.transpose(weights_ref[...])
    for cols in column_tiles(landed_refs[0].shape[1], 512):
        landed = jnp.concatenate([ref[:, cols] for ref in landed_refs], axis=0)
        total = dot(weights, landed).astype(jnp.bfloat16)
        start = 0
        for ref in out_refs:
            ref[:, cols] = total[start : start + ref.shape[0]]
            start += ref.shape[0]


def combine(weights, landed, sizes):
    width = landed[0].shape[1]
    return pl.pallas_call(
        combine_kernel,
        out_shape=[jax.ShapeDtypeStruct((size, width), jnp.bfloat16) for size in sizes],
        in_specs=[VMEM] * (1 + Y),
        out_specs=[VMEM] * len(sizes),
        name="combine",
    )(weights, *landed)


def wide(value):
    return value.astype(jnp.float32)


def section(first, arrived, fresh, gain, router, picks, ids, w_gate, w_up, w_down):
    tokens = arrived.shape[0]
    current, packed = prepare(first, arrived, fresh, gain, router, picks)
    near = jnp.concatenate([packed, to_other_core(packed)], axis=0)
    one = outward(near)
    two = outward(one)
    three = outward(two)
    four = outward(three[:tokens])
    chunks = [
        [near, one, to_other_core(one)],
        [two, to_other_core(two)],
        [three, to_other_core(three)],
        [four, to_other_core(four)],
    ]
    rows, weights = [], []
    for chunk in chunks:
        sent, weight = dispatch(ids, chunk, tokens)
        rows.append([along_y(value, step) for step, value in enumerate(sent)])
        weights.append(weight)
    early = run_experts(rows[0] + rows[1], w_gate, w_up, w_down)
    late = run_experts(rows[2] + rows[3], w_gate, w_up, w_down)
    outputs = [early[:Y], early[Y:], late[:Y], late[Y:]]
    parts = []
    for chunk, weight, output in zip(chunks, weights, outputs):
        landed = [along_y(value, -step) for step, value in enumerate(output)]
        parts.append(combine(weight, landed, [value.shape[0] for value in chunk]))
    part = [wide(kept) + wide(to_other_core(sent)) for *_, kept, sent in parts]
    stream = homeward(part[3].astype(jnp.bfloat16))
    total = part[2] + jnp.pad(wide(stream), ((0, tokens), (0, 0)))
    stream = homeward(total.astype(jnp.bfloat16))
    stream = homeward((part[1] + wide(stream)).astype(jnp.bfloat16))
    stream = homeward((part[0] + wide(stream)).astype(jnp.bfloat16))
    held = wide(stream) + wide(parts[0][0])
    other = to_other_core(held[tokens:].astype(jnp.bfloat16))
    return (wide(current) + held[:tokens] + wide(other)).astype(jnp.bfloat16)


def shards(entering, fresh, w_gate, w_up, w_down, router, gain, routes):
    at_start = (lax.axis_index("segment") == 0).astype(jnp.int32).reshape(1)
    never = jnp.zeros((1,), jnp.int32)
    place, core = lax.axis_index("expert"), lax.axis_index("dp")
    z, y = place // Y, place % Y
    ids = (z * Y + (y + jnp.arange(Y, dtype=jnp.int32)) % Y) * C + core
    router_rows = jnp.transpose(router[0])
    picks = jnp.transpose(routes[0], (0, 2, 1))
    results = []
    count = lax.axis_size("segment")
    for step in range(routes.shape[1]):
        if step == 0:
            first, arrived, other = never, entering[0], entering[0]
        else:
            arrived = lax.ppermute(results[-1], "segment", [(i, i + 1) for i in range(count - 1)])
            first, other = at_start, fresh[step - 1]
        results.append(
            section(first, arrived, other, gain, router_rows, picks[step], ids, w_gate[0, 0], w_up[0, 0], w_down[0, 0])
        )
    return jnp.stack(results)[None]


def solution(mesh):
    tokens = P("segment", ("expert", "dp"), None)
    weights = P("segment", ("expert", "dp"), None, None)
    in_specs = (
        tokens, P(None, ("expert", "dp"), None), weights, weights, weights,
        P("segment", None, None), P("segment", None), P("segment", None, ("expert", "dp"), None),
    )
    out_specs = P("segment", None, ("expert", "dp"), None)
    return jax.shard_map(shards, mesh=mesh, in_specs=in_specs, out_specs=out_specs, check_vma=False)
```

```python
import jax
import jax.numpy as jnp
from jax import lax
from jax.experimental import pallas as pl
from jax.experimental.pallas import tpu as pltpu
from jax.sharding import PartitionSpec as P

CAP = 8
GROUP = ("expert", "dp")


def dot(lhs, rhs, lhs_dim=1, rhs_dim=0):
    return lax.dot_general(
        lhs, rhs, (((lhs_dim,), (rhs_dim,)), ((), ())), preferred_element_type=jnp.float32
    )


def column_tiles(width, tile):
    return [slice(start, min(start + tile, width)) for start in range(0, width, tile)]


def prepare_kernel(step, first_ref, arrived_ref, fresh_ref, gain_ref, router_ref, picks_ref,
                   current_ref, rows_ref, weights_ref):
    tokens, width = current_ref.shape
    experts = router_ref.shape[0]
    picked = arrived_ref[...]
    current = jnp.where(first_ref[0] == 1, fresh_ref[...], picked)
    current_ref[...] = current
    values = current.astype(jnp.float32)
    inv_scale = lax.rsqrt(jnp.mean(values * values, axis=1, keepdims=True) + 1e-06)
    normed = (values * inv_scale * gain_ref[...]).astype(jnp.bfloat16)
    logits = dot(router_ref[...], normed, 1, 1)
    expert_ids = lax.broadcasted_iota(jnp.int32, (experts, tokens), 0)
    chosen = jnp.zeros((experts, tokens), jnp.float32)
    for choice in range(picks_ref.shape[0]):
        chosen = chosen + jnp.where(picks_ref[choice, step : step + 1, :] == expert_ids, 1.0, 0.0)
    scores = chosen / (1.0 + jnp.exp(-logits))
    mixing = scores / jnp.sum(scores, axis=0, keepdims=True)
    before = jnp.where(
        lax.broadcasted_iota(jnp.int32, (tokens, tokens), 0)
        < lax.broadcasted_iota(jnp.int32, (tokens, tokens), 1), 1.0, 0.0
    ).astype(jnp.bfloat16)
    rank = dot(chosen.astype(jnp.bfloat16), before)
    slot = jnp.where(chosen > 0.0, rank, float(CAP))
    slot_rows = jnp.broadcast_to(slot[:, None, :], (experts, CAP, tokens))
    slot_ids = lax.broadcasted_iota(jnp.int32, (experts, CAP, tokens), 1).astype(jnp.float32)
    here = slot_rows == slot_ids
    pick = jnp.where(here, 1.0, 0.0).reshape(experts * CAP, tokens).astype(jnp.bfloat16)
    mixed = jnp.where(here, jnp.broadcast_to(mixing[:, None, :], here.shape), 0.0)
    weights_ref[...] = mixed.reshape(experts * CAP, tokens).astype(jnp.bfloat16)
    for cols in column_tiles(width, 512):
        rows_ref[:, cols] = dot(pick, normed[:, cols]).astype(jnp.bfloat16)


def prepare(step, first, arrived, fresh, gain, router, picks):
    tokens, width = arrived.shape
    slots = router.shape[0] * CAP
    vmem = pl.BlockSpec(memory_space=pltpu.VMEM)
    return pl.pallas_call(
        lambda *refs: prepare_kernel(step, *refs),
        out_shape=(
            jax.ShapeDtypeStruct((tokens, width), jnp.bfloat16),
            jax.ShapeDtypeStruct((slots, width), jnp.bfloat16),
            jax.ShapeDtypeStruct((slots, tokens), jnp.bfloat16),
        ),
        in_specs=[pl.BlockSpec(memory_space=pltpu.SMEM)] + [vmem] * 5,
        out_specs=(vmem, vmem, vmem),
        name="prepare",
    )(first, arrived, fresh, gain, router, picks)


def experts_kernel(rows_ref, gate_hbm, up_hbm, down_hbm, out_ref, gate_ref, up_ref, down_ref, hidden_ref, arrived):
    width, inner = gate_ref.shape
    tiles = column_tiles(inner, 256)
    copies = []
    for index, cols in enumerate(tiles):
        for which, (source, target) in enumerate(((gate_hbm, gate_ref), (up_hbm, up_ref))):
            copies.append(pltpu.make_async_copy(source.at[:, cols], target.at[:, cols], arrived.at[2 * index + which]))
    last = pltpu.make_async_copy(down_hbm, down_ref, arrived.at[2 * len(tiles)])
    for copy in copies:
        copy.start()
    last.start()
    for index, cols in enumerate(tiles):
        copies[2 * index].wait()
        gate = dot(rows_ref[...], gate_ref[:, cols])
        copies[2 * index + 1].wait()
        up = dot(rows_ref[...], up_ref[:, cols])
        hidden_ref[:, cols] = (gate / (1.0 + jnp.exp(-gate)) * up).astype(jnp.bfloat16)
    last.wait()
    for cols in column_tiles(width, 512):
        out_ref[:, cols] = dot(hidden_ref[...], down_ref[:, cols]).astype(jnp.bfloat16)


def run_experts(rows, w_gate, w_up, w_down):
    count, width = rows.shape
    hidden = w_gate.shape[1]
    vmem, hbm = pl.BlockSpec(memory_space=pltpu.VMEM), pl.BlockSpec(memory_space=pl.ANY)
    return pl.pallas_call(
        experts_kernel,
        out_shape=jax.ShapeDtypeStruct((count, width), jnp.bfloat16),
        in_specs=[vmem, hbm, hbm, hbm],
        out_specs=vmem,
        scratch_shapes=[
            pltpu.VMEM((width, hidden), jnp.bfloat16),
            pltpu.VMEM((width, hidden), jnp.bfloat16),
            pltpu.VMEM((hidden, width), jnp.bfloat16),
            pltpu.VMEM((count, hidden), jnp.bfloat16),
            pltpu.SemaphoreType.DMA((2 * len(column_tiles(hidden, 256)) + 1,)),
        ],
        compiler_params=pltpu.CompilerParams(vmem_limit_bytes=40 << 20),
        name="experts",
    )(rows, w_gate, w_up, w_down)


def combine_kernel(earlier, current_ref, weights_ref, landed_ref, *refs):
    out_ref = refs[-1]
    weights = jnp.transpose(weights_ref[...])
    for index in range(earlier):
        out_ref[index] = refs[index][0]
    for cols in column_tiles(out_ref.shape[2], 512):
        total = current_ref[:, cols].astype(jnp.float32) + dot(weights, landed_ref[:, cols])
        out_ref[earlier, :, cols] = total.astype(jnp.bfloat16)


def combine(current, weights, landed, *results):
    vmem = pl.BlockSpec(memory_space=pltpu.VMEM)
    return pl.pallas_call(
        lambda *refs: combine_kernel(len(results), *refs),
        out_shape=jax.ShapeDtypeStruct((len(results) + 1, *current.shape), jnp.bfloat16),
        in_specs=[vmem] * (3 + len(results)),
        out_specs=vmem,
        name="combine",
    )(current, weights, landed, *results)


def exchange(rows):
    count, width = rows.shape
    parts = rows.reshape(count // CAP, CAP, width)
    moved = lax.all_to_all(parts, GROUP, split_axis=0, concat_axis=0, tiled=True)
    return moved.reshape(count, width)


def shards(entering, fresh, w_gate, w_up, w_down, router, gain, routes):
    at_start = (lax.axis_index("segment") == 0).astype(jnp.int32).reshape(1)
    never = jnp.zeros((1,), jnp.int32)
    router_rows = jnp.transpose(router[0])
    picks = jnp.transpose(routes[0], (2, 0, 1))
    w_gate, w_up, w_down = (
        pltpu.with_memory_space_constraint(value[0, 0], pltpu.HBM) for value in (w_gate, w_up, w_down)
    )
    results = []
    count = lax.axis_size("segment")
    steps = routes.shape[1]
    for step in range(steps):
        if step == 0:
            first, arrived, other = never, entering[0], entering[0]
        else:
            arrived = lax.ppermute(results[-1][0], "segment", [(i, i + 1) for i in range(count - 1)])
            first, other = at_start, fresh[step - 1]
        current, rows, weights = prepare(step, first, arrived, other, gain, router_rows, picks)
        landed = exchange(run_experts(exchange(rows), w_gate, w_up, w_down))
        results.append(combine(current, weights, landed, *(results if step == steps - 1 else [])))
    return results[-1][None]


def solution(mesh):
    tokens = P("segment", ("expert", "dp"), None)
    weights = P("segment", ("expert", "dp"), None, None)
    in_specs = (
        tokens, P(None, ("expert", "dp"), None), weights, weights, weights,
        P("segment", None, None), P("segment", None), P("segment", None, ("expert", "dp"), None),
    )
    out_specs = P("segment", None, ("expert", "dp"), None)
    return jax.shard_map(shards, mesh=mesh, in_specs=in_specs, out_specs=out_specs, check_vma=False)
```

```python
import jax
import jax.numpy as jnp
from jax import lax
from jax.experimental import pallas as pl
from jax.experimental.pallas import tpu as pltpu
from jax.sharding import PartitionSpec as P

CAP = 8
GROUP = ("expert", "dp")


def dot(lhs, rhs, lhs_dim=1, rhs_dim=0):
    return lax.dot_general(
        lhs, rhs, (((lhs_dim,), (rhs_dim,)), ((), ())), preferred_element_type=jnp.float32
    )


def column_tiles(width, tile):
    return [slice(start, min(start + tile, width)) for start in range(0, width, tile)]


def prepare_kernel(step, first_ref, arrived_ref, fresh_ref, gain_ref, router_ref, picks_ref,
                   current_ref, rows_ref, weights_ref):
    tokens, width = current_ref.shape
    experts = router_ref.shape[0]
    picked = arrived_ref[...]
    current = jnp.where(first_ref[0] == 1, fresh_ref[...], picked)
    current_ref[...] = current
    values = current.astype(jnp.float32)
    inv_scale = lax.rsqrt(jnp.mean(values * values, axis=1, keepdims=True) + 1e-06)
    normed = (values * inv_scale * gain_ref[...]).astype(jnp.bfloat16)
    logits = dot(router_ref[...], normed, 1, 1)
    expert_ids = lax.broadcasted_iota(jnp.int32, (experts, tokens), 0)
    chosen = jnp.zeros((experts, tokens), jnp.float32)
    for choice in range(picks_ref.shape[0]):
        chosen = chosen + jnp.where(picks_ref[choice, step : step + 1, :] == expert_ids, 1.0, 0.0)
    scores = chosen / (1.0 + jnp.exp(-logits))
    mixing = scores / jnp.sum(scores, axis=0, keepdims=True)
    before = jnp.where(
        lax.broadcasted_iota(jnp.int32, (tokens, tokens), 0)
        < lax.broadcasted_iota(jnp.int32, (tokens, tokens), 1), 1.0, 0.0
    ).astype(jnp.bfloat16)
    rank = dot(chosen.astype(jnp.bfloat16), before)
    slot = jnp.where(chosen > 0.0, rank, float(CAP))
    slot_rows = jnp.broadcast_to(slot[:, None, :], (experts, CAP, tokens))
    slot_ids = lax.broadcasted_iota(jnp.int32, (experts, CAP, tokens), 1).astype(jnp.float32)
    here = slot_rows == slot_ids
    pick = jnp.where(here, 1.0, 0.0).reshape(experts * CAP, tokens).astype(jnp.bfloat16)
    mixed = jnp.where(here, jnp.broadcast_to(mixing[:, None, :], here.shape), 0.0)
    weights_ref[...] = mixed.reshape(experts * CAP, tokens).astype(jnp.bfloat16)
    for cols in column_tiles(width, 512):
        rows_ref[:, cols] = dot(pick, normed[:, cols]).astype(jnp.bfloat16)


def prepare(step, first, arrived, fresh, gain, router, picks):
    tokens, width = arrived.shape
    slots = router.shape[0] * CAP
    vmem = pl.BlockSpec(memory_space=pltpu.VMEM)
    return pl.pallas_call(
        lambda *refs: prepare_kernel(step, *refs),
        out_shape=(
            jax.ShapeDtypeStruct((tokens, width), jnp.bfloat16),
            jax.ShapeDtypeStruct((slots, width), jnp.bfloat16),
            jax.ShapeDtypeStruct((slots, tokens), jnp.bfloat16),
        ),
        in_specs=[pl.BlockSpec(memory_space=pltpu.SMEM)] + [vmem] * 5,
        out_specs=(vmem, vmem, vmem),
        name="prepare",
    )(first, arrived, fresh, gain, router, picks)


def experts_kernel(rows_ref, gate_hbm, up_hbm, down_hbm, out_ref,
                   gate_ref, up_ref, down_ref, gated_ref, upper_ref, hidden_ref, arrived):
    width, inner = gate_ref.shape
    parts, tiles = column_tiles(width, 512), column_tiles(inner, 256)
    copies = []
    for index, part in enumerate(parts):
        for which, (source, target) in enumerate(((gate_hbm, gate_ref), (up_hbm, up_ref))):
            copies.append(pltpu.make_async_copy(source.at[part, :], target.at[part, :], arrived.at[2 * index + which]))
    last = pltpu.make_async_copy(down_hbm, down_ref, arrived.at[2 * len(parts)])
    for copy in copies:
        copy.start()
    last.start()
    for index, part in enumerate(parts):
        copies[2 * index].wait()
        copies[2 * index + 1].wait()
        rows = rows_ref[:, part]
        for cols in tiles:
            gate, up = dot(rows, gate_ref[part, cols]), dot(rows, up_ref[part, cols])
            if index > 0:
                gate, up = gated_ref[:, cols] + gate, upper_ref[:, cols] + up
            if index < len(parts) - 1:
                gated_ref[:, cols], upper_ref[:, cols] = gate, up
            else:
                hidden_ref[:, cols] = (gate / (1.0 + jnp.exp(-gate)) * up).astype(jnp.bfloat16)
    last.wait()
    hidden = hidden_ref[...]
    for cols in column_tiles(width, 512):
        out_ref[:, cols] = dot(hidden, down_ref[:, cols]).astype(jnp.bfloat16)


def run_experts(rows, w_gate, w_up, w_down):
    count, width = rows.shape
    hidden = w_gate.shape[1]
    vmem, hbm = pl.BlockSpec(memory_space=pltpu.VMEM), pl.BlockSpec(memory_space=pl.ANY)
    return pl.pallas_call(
        experts_kernel,
        out_shape=jax.ShapeDtypeStruct((count, width), jnp.bfloat16),
        in_specs=[vmem, hbm, hbm, hbm],
        out_specs=vmem,
        scratch_shapes=[
            pltpu.VMEM((width, hidden), jnp.bfloat16),
            pltpu.VMEM((width, hidden), jnp.bfloat16),
            pltpu.VMEM((hidden, width), jnp.bfloat16),
            pltpu.VMEM((count, hidden), jnp.float32),
            pltpu.VMEM((count, hidden), jnp.float32),
            pltpu.VMEM((count, hidden), jnp.bfloat16),
            pltpu.SemaphoreType.DMA((2 * len(column_tiles(width, 512)) + 1,)),
        ],
        compiler_params=pltpu.CompilerParams(vmem_limit_bytes=44 << 20),
        name="experts",
    )(rows, w_gate, w_up, w_down)


def combine_kernel(earlier, current_ref, weights_ref, landed_ref, *refs):
    out_ref = refs[-1]
    weights = jnp.transpose(weights_ref[...])
    for index in range(earlier):
        out_ref[index] = refs[index][0]
    for cols in column_tiles(out_ref.shape[2], 512):
        total = current_ref[:, cols].astype(jnp.float32) + dot(weights, landed_ref[:, cols])
        out_ref[earlier, :, cols] = total.astype(jnp.bfloat16)


def combine(current, weights, landed, *results):
    vmem = pl.BlockSpec(memory_space=pltpu.VMEM)
    return pl.pallas_call(
        lambda *refs: combine_kernel(len(results), *refs),
        out_shape=jax.ShapeDtypeStruct((len(results) + 1, *current.shape), jnp.bfloat16),
        in_specs=[vmem] * (3 + len(results)),
        out_specs=vmem,
        name="combine",
    )(current, weights, landed, *results)


def exchange(rows):
    count, width = rows.shape
    parts = rows.reshape(count // CAP, CAP, width)
    moved = lax.all_to_all(parts, GROUP, split_axis=0, concat_axis=0, tiled=True)
    return moved.reshape(count, width)


def shards(entering, fresh, w_gate, w_up, w_down, router, gain, routes):
    at_start = (lax.axis_index("segment") == 0).astype(jnp.int32).reshape(1)
    never = jnp.zeros((1,), jnp.int32)
    router_rows = jnp.transpose(router[0])
    picks = jnp.transpose(routes[0], (2, 0, 1))
    w_gate, w_up, w_down = (
        pltpu.with_memory_space_constraint(value[0, 0], pltpu.HBM) for value in (w_gate, w_up, w_down)
    )
    results = []
    count = lax.axis_size("segment")
    steps = routes.shape[1]
    for step in range(steps):
        if step == 0:
            first, arrived, other = never, entering[0], entering[0]
        else:
            arrived = lax.ppermute(results[-1][0], "segment", [(i, i + 1) for i in range(count - 1)])
            first, other = at_start, fresh[step - 1]
        current, rows, weights = prepare(step, first, arrived, other, gain, router_rows, picks)
        landed = exchange(run_experts(exchange(rows), w_gate, w_up, w_down))
        results.append(combine(current, weights, landed, *(results if step == steps - 1 else [])))
    return results[-1][None]


def solution(mesh):
    tokens = P("segment", ("expert", "dp"), None)
    weights = P("segment", ("expert", "dp"), None, None)
    in_specs = (
        tokens, P(None, ("expert", "dp"), None), weights, weights, weights,
        P("segment", None, None), P("segment", None), P("segment", None, ("expert", "dp"), None),
    )
    out_specs = P("segment", None, ("expert", "dp"), None)
    return jax.shard_map(shards, mesh=mesh, in_specs=in_specs, out_specs=out_specs, check_vma=False)
```

```python
import jax
import jax.numpy as jnp
from jax import lax
from jax.experimental import pallas as pl
from jax.experimental.pallas import tpu as pltpu
from jax.sharding import PartitionSpec as P

CAP = 8
LANES = 128
GROUP = ("expert", "dp")
Z, Y, C = 8, 4, 2
VMEM = pl.BlockSpec(memory_space=pltpu.VMEM)
BRIEF = pl.CostEstimate(flops=1000, transcendentals=0, bytes_accessed=1000)
SMEM = pl.BlockSpec(memory_space=pltpu.SMEM)


def dot(lhs, rhs, lhs_dim=1, rhs_dim=0):
    return lax.dot_general(
        lhs, rhs, (((lhs_dim,), (rhs_dim,)), ((), ())), preferred_element_type=jnp.float32
    )


def column_tiles(width, tile):
    return [slice(start, min(start + tile, width)) for start in range(0, width, tile)]


def iota(shape, dim):
    return lax.broadcasted_iota(jnp.int32, shape, dim)


def move(value, target):
    pairs = []
    for z in range(Z):
        for y in range(Y):
            for core in range(C):
                to_z, to_y, to_core = target(z, y, core)
                pairs.append(((z * Y + y) * C + core, ((to_z % Z) * Y + to_y % Y) * C + to_core))
    return lax.ppermute(value, GROUP, pairs)


def to_other_core(value):
    return move(value, lambda z, y, core: (z, y, 1 - core))


def along_y(value, steps):
    return value if steps == 0 else move(value, lambda z, y, core: (z, y + steps, core))


def along_z(value, steps):
    return move(value, lambda z, y, core: (z + steps, y, core))


def after(value, *others):
    return lax.optimization_barrier((value, *others))[0]


def prepare_kernel(step, first_ref, arrived_ref, fresh_ref, gain_ref, router_ref, picks_ref,
                   current_ref, packed_ref, weights_ref):
    tokens, width = current_ref.shape
    experts = router_ref.shape[0]
    current = jnp.where(first_ref[0] == 1, fresh_ref[...], arrived_ref[...])
    current_ref[...] = current
    values = current.astype(jnp.float32)
    inv_scale = lax.rsqrt(jnp.mean(values * values, axis=1, keepdims=True) + 1e-06)
    normed = (values * inv_scale * gain_ref[...]).astype(jnp.bfloat16)
    packed_ref[:, :width] = normed
    logits = dot(normed, router_ref[...], 1, 1)
    expert_ids = iota((experts, tokens), 0)
    chosen_rows = jnp.zeros((experts, tokens), jnp.float32)
    for choice in range(picks_ref.shape[0]):
        chosen_rows += jnp.where(picks_ref[choice, step : step + 1, :] == expert_ids, 1.0, 0.0)
    chosen_rows = chosen_rows.astype(jnp.bfloat16)
    row, column = iota((tokens, tokens), 0), iota((tokens, tokens), 1)
    chosen = dot(jnp.where(row == column, 1.0, 0.0).astype(jnp.bfloat16), chosen_rows, 1, 1)
    rank = dot(jnp.where(column < row, 1.0, 0.0).astype(jnp.bfloat16), chosen_rows, 1, 1)
    scores = chosen / (1.0 + jnp.exp(-logits))
    mixing = (scores / jnp.sum(scores, axis=1, keepdims=True)).astype(jnp.bfloat16)
    slot = jnp.where(chosen > 0.0, rank, float(CAP)).astype(jnp.bfloat16)
    packed_ref[:, width:] = jnp.concatenate([slot.astype(jnp.float32), mixing.astype(jnp.float32)], axis=1).astype(jnp.bfloat16)
    places = experts * CAP
    spread = jnp.where(iota((experts, places), 1) // CAP == iota((experts, places), 0), 1.0, 0.0).astype(jnp.bfloat16)
    here = dot(slot, spread) == (iota((tokens, places), 1) % CAP).astype(jnp.float32)
    weights_ref[...] = jnp.where(here, dot(mixing, spread), 0.0).astype(jnp.bfloat16)


def prepare(step, first, arrived, fresh, gain, router, picks):
    tokens, width = arrived.shape
    return pl.pallas_call(
        lambda *refs: prepare_kernel(step, *refs),
        out_shape=(
            jax.ShapeDtypeStruct((tokens, width), jnp.bfloat16),
            jax.ShapeDtypeStruct((tokens, width + LANES), jnp.bfloat16),
            jax.ShapeDtypeStruct((tokens, router.shape[0] * CAP), jnp.bfloat16),
        ),
        in_specs=[SMEM] + [VMEM] * 5,
        out_specs=(VMEM, VMEM, VMEM),
        cost_estimate=BRIEF,
        name="prepare",
    )(first, arrived, fresh, gain, router, picks)


def stacked(pieces):
    return jnp.concatenate([piece.astype(jnp.float32) for piece in pieces], axis=0).astype(jnp.bfloat16)


def dispatch_kernel(block, count, ids_ref, *refs):
    packed_refs, row_refs = refs[:count], refs[count:]
    width = row_refs[0].shape[1]
    rows = row_refs[0].shape[0] // C
    notes = jnp.concatenate([ref[:, width:] for ref in packed_refs], axis=0)
    tokens = notes.shape[0]
    line, lane = iota((2 * Y * C, LANES), 0), iota((2 * Y * C, LANES), 1)
    select = jnp.zeros((2 * Y * C, LANES), jnp.float32)
    for place in range(Y * C):
        hit = (line == place) & (lane == ids_ref[place])
        select = jnp.where(hit, 1.0, select)
    picked = dot(select.astype(jnp.bfloat16), notes, 1, 1)
    row, token = iota((rows, tokens), 0), iota((rows, tokens), 1)
    code = jnp.where(token // block == row // CAP, row % CAP, -1).astype(jnp.float32)
    picks = []
    for place in range(Y * C):
        here = jnp.broadcast_to(picked[place : place + 1, :], (rows, tokens)) == code
        picks.append(jnp.where(here, 1.0, 0.0))
    pick = jnp.concatenate(picks, axis=0).astype(jnp.bfloat16)

    for cols in column_tiles(width, 512):
        values = jnp.concatenate([ref[:, cols] for ref in packed_refs], axis=0)
        result = dot(pick, values).astype(jnp.bfloat16)
        for step in range(Y):
            row_refs[step][:, cols] = result[step * C * rows : (step + 1) * C * rows]


def dispatch(ids, packed, block):
    width = packed[0].shape[1] - LANES
    tokens = sum(value.shape[0] for value in packed)
    rows = tokens // block * CAP
    return pl.pallas_call(
        lambda *refs: dispatch_kernel(block, len(packed), *refs),
        out_shape=[jax.ShapeDtypeStruct((C * rows, width), jnp.bfloat16)] * Y,
        in_specs=[SMEM] + [VMEM] * len(packed),
        out_specs=[VMEM] * Y,
        cost_estimate=BRIEF,
        name="dispatch",
    )(ids, *packed)


def swapped_half(arrays):
    half = arrays[0].shape[0] // C
    return to_other_core(jnp.concatenate([value[half:] for value in arrays], axis=0))


def experts_kernel(groups, places_ref, *refs):
    row_refs = [refs[index * (Y + 1) : (index + 1) * (Y + 1)] for index in range(groups)]
    gate_hbm, up_hbm, down_hbm, out_ref = refs[groups * (Y + 1) : groups * (Y + 1) + 4]
    gate_ref, up_ref, down_ref, gated_ref, upper_ref, hidden_ref, arrived = refs[groups * (Y + 1) + 4 :]
    width, inner = gate_ref.shape
    parts, tiles = column_tiles(width, 512), column_tiles(inner, 256)
    copies = []
    for index, part in enumerate(parts):
        for which, (source, target) in enumerate(((gate_hbm, gate_ref), (up_hbm, up_ref))):
            copies.append(pltpu.make_async_copy(source.at[part, :], target.at[part, :], arrived.at[2 * index + which]))
    last = pltpu.make_async_copy(down_hbm, down_ref, arrived.at[2 * len(parts)])
    for copy in copies:
        copy.start()
    last.start()
    for index, part in enumerate(parts):
        pieces = []
        for group in row_refs:
            pieces += [ref[: ref.shape[0] // C, part] for ref in group[:Y]] + [group[Y][:, part]]
        rows = stacked(pieces)
        copies[2 * index].wait()
        copies[2 * index + 1].wait()
        for cols in tiles:
            gate, up = dot(rows, gate_ref[part, cols]), dot(rows, up_ref[part, cols])
            if index > 0:
                gate, up = gated_ref[:, cols] + gate, upper_ref[:, cols] + up
            if index < len(parts) - 1:
                gated_ref[:, cols], upper_ref[:, cols] = gate, up
            else:
                hidden_ref[:, cols] = (gate / (1.0 + jnp.exp(-gate)) * up).astype(jnp.bfloat16)
    last.wait()
    hidden = hidden_ref[...]
    for cols in column_tiles(width, 512):
        result = dot(hidden, down_ref[:, cols])
        for place in range(out_ref.shape[0]):
            piece = result[place * CAP : (place + 1) * CAP].astype(jnp.bfloat16)
            out_ref[pl.ds(places_ref[place], 1), :, cols] = piece[None]


def run_experts(groups, places, w_gate, w_up, w_down):
    width, hidden = w_gate.shape
    operands = []
    for arrays in groups:
        operands += [*arrays, swapped_half(arrays)]
    count = places.shape[0] * CAP
    return pl.pallas_call(
        lambda *refs: experts_kernel(len(groups), *refs),
        out_shape=jax.ShapeDtypeStruct((places.shape[0], CAP, width), jnp.bfloat16),
        in_specs=[SMEM] + [VMEM] * len(operands) + [pl.BlockSpec(memory_space=pl.ANY)] * 3,
        out_specs=VMEM,
        scratch_shapes=[
            pltpu.VMEM((width, hidden), jnp.bfloat16),
            pltpu.VMEM((width, hidden), jnp.bfloat16),
            pltpu.VMEM((hidden, width), jnp.bfloat16),
            pltpu.VMEM((count, hidden), jnp.float32),
            pltpu.VMEM((count, hidden), jnp.float32),
            pltpu.VMEM((count, hidden), jnp.bfloat16),
            pltpu.SemaphoreType.DMA((2 * len(column_tiles(width, 512)) + 1,)),
        ],
        compiler_params=pltpu.CompilerParams(vmem_limit_bytes=44 << 20),
        cost_estimate=BRIEF,
        name="experts",
    )(places, *operands, w_gate, w_up, w_down)


def combine_kernel(earlier, current_ref, weights_ref, landed_ref, *refs):
    out_ref = refs[-1]
    weights = weights_ref[...]
    for index in range(earlier):
        out_ref[index] = refs[index][0]
    for cols in column_tiles(out_ref.shape[2], 512):
        total = current_ref[:, cols].astype(jnp.float32) + dot(weights, landed_ref[:, cols])
        out_ref[earlier, :, cols] = total.astype(jnp.bfloat16)


def combine(current, weights, landed, *results):
    return pl.pallas_call(
        lambda *refs: combine_kernel(len(results), *refs),
        out_shape=jax.ShapeDtypeStruct((len(results) + 1, *current.shape), jnp.bfloat16),
        in_specs=[VMEM] * (3 + len(results)),
        out_specs=VMEM,
        cost_estimate=BRIEF,
        name="combine",
    )(current, weights, landed, *results)


NEAR, FAR = (0, -1, 1, -2, 2), (-3, 3, 4)


def section(packed, ids, places, w_gate, w_up, w_down):
    tokens = packed.shape[0]
    part = tokens // 2
    below, above = [packed], [packed]
    for _ in range(2):
        below.append(along_z(below[-1], 1))
        above.append(along_z(above[-1], -1))
    near_rows = dispatch(ids, [packed, below[1], above[1], below[2], above[2]], tokens)
    below.append(along_z(below[2], 1))
    above.append(along_z(above[2], -1))
    third = after(below[3], near_rows[0]), after(above[3], near_rows[0])
    far = [below[3], above[3], along_z(third[0][:part], 1), along_z(third[1][part:], -1)]
    far_rows = dispatch(ids, far, tokens)
    near_there = [along_y(value, step) for step, value in enumerate(near_rows)]
    near_there = [after(value, far_rows[0]) for value in near_there]
    far_there = [along_y(value, step) for step, value in enumerate(far_rows)]
    outputs = run_experts([near_there, far_there], places, w_gate, w_up, w_down)
    landed = lax.all_to_all(outputs, GROUP, split_axis=0, concat_axis=0, tiled=True)
    return landed.reshape(-1, landed.shape[-1])


def shards(entering, fresh, w_gate, w_up, w_down, router, gain, routes):
    at_start = (lax.axis_index("segment") == 0).astype(jnp.int32).reshape(1)
    never = jnp.zeros((1,), jnp.int32)
    place, core = lax.axis_index("expert"), lax.axis_index("dp")
    z, y = place // Y, place % Y
    steps = jnp.arange(Y * C, dtype=jnp.int32)
    ids = (z * Y + (y + steps // C) % Y) * C + (core + steps % C) % C
    order = [(block, step, side) for group in (NEAR, FAR) for side in range(C) for step in range(Y) for block in group]
    block, step, side = (jnp.array(column, jnp.int32) for column in zip(*order))
    places = ((z + block + Z) % Z * Y + (y - step + Y) % Y) * C + (core + side) % C
    router_rows = jnp.transpose(router[0])
    picks = jnp.transpose(routes[0], (2, 0, 1))
    w_gate, w_up, w_down = (
        pltpu.with_memory_space_constraint(value[0, 0], pltpu.HBM) for value in (w_gate, w_up, w_down)
    )
    results = []
    count = lax.axis_size("segment")
    for index in range(routes.shape[1]):
        if index == 0:
            first, arrived, other = never, entering[0], entering[0]
        else:
            arrived = lax.ppermute(results[-1][0], "segment", [(i, i + 1) for i in range(count - 1)])
            first, other = at_start, fresh[index - 1]
        current, packed, weights = prepare(index, first, arrived, other, gain, router_rows, picks)
        landed = section(packed, ids, places, w_gate, w_up, w_down)
        results.append(combine(current, weights, landed, *(results if index == routes.shape[1] - 1 else [])))
    return results[-1][None]


def solution(mesh):
    tokens = P("segment", ("expert", "dp"), None)
    weights = P("segment", ("expert", "dp"), None, None)
    in_specs = (
        tokens, P(None, ("expert", "dp"), None), weights, weights, weights,
        P("segment", None, None), P("segment", None), P("segment", None, ("expert", "dp"), None),
    )
    out_specs = P("segment", None, ("expert", "dp"), None)
    return jax.shard_map(shards, mesh=mesh, in_specs=in_specs, out_specs=out_specs, check_vma=False)
```

```python
import jax
import jax.numpy as jnp
from jax import lax
from jax.experimental import pallas as pl
from jax.experimental.pallas import tpu as pltpu
from jax.sharding import PartitionSpec as P

CAP = 8
LANES = 128
GROUP = ("expert", "dp")
Z, Y, C = 8, 4, 2
VMEM = pl.BlockSpec(memory_space=pltpu.VMEM)
BRIEF = pl.CostEstimate(flops=1000, transcendentals=0, bytes_accessed=1000)
SMEM = pl.BlockSpec(memory_space=pltpu.SMEM)


def dot(lhs, rhs, lhs_dim=1, rhs_dim=0):
    return lax.dot_general(
        lhs, rhs, (((lhs_dim,), (rhs_dim,)), ((), ())), preferred_element_type=jnp.float32
    )


def column_tiles(width, tile):
    return [slice(start, min(start + tile, width)) for start in range(0, width, tile)]


def iota(shape, dim):
    return lax.broadcasted_iota(jnp.int32, shape, dim)


def move(value, target):
    pairs = []
    for z in range(Z):
        for y in range(Y):
            for core in range(C):
                to_z, to_y, to_core = target(z, y, core)
                pairs.append(((z * Y + y) * C + core, ((to_z % Z) * Y + to_y % Y) * C + to_core))
    return lax.ppermute(value, GROUP, pairs)


def to_other_core(value):
    return move(value, lambda z, y, core: (z, y, 1 - core))


def along_y(value, steps):
    return value if steps == 0 else move(value, lambda z, y, core: (z, y + steps, core))


def along_z(value, steps):
    return move(value, lambda z, y, core: (z + steps, y, core))


def after(value, *others):
    return lax.optimization_barrier((value, *others))[0]


def prepare_kernel(step, first_ref, arrived_ref, fresh_ref, gain_ref, router_ref, picks_ref,
                   current_ref, packed_ref, weights_ref):
    tokens, width = current_ref.shape
    experts = router_ref.shape[0]
    current = jnp.where(first_ref[0] == 1, fresh_ref[...], arrived_ref[...])
    current_ref[...] = current
    values = current.astype(jnp.float32)
    inv_scale = lax.rsqrt(jnp.mean(values * values, axis=1, keepdims=True) + 1e-06)
    normed = (values * inv_scale * gain_ref[...]).astype(jnp.bfloat16)
    packed_ref[:, :width] = normed
    logits = dot(normed, router_ref[...], 1, 1)
    expert_ids = iota((experts, tokens), 0)
    chosen_rows = jnp.zeros((experts, tokens), jnp.float32)
    for choice in range(picks_ref.shape[0]):
        chosen_rows += jnp.where(picks_ref[choice, step : step + 1, :] == expert_ids, 1.0, 0.0)
    chosen_rows = chosen_rows.astype(jnp.bfloat16)
    row, column = iota((tokens, tokens), 0), iota((tokens, tokens), 1)
    chosen = dot(jnp.where(row == column, 1.0, 0.0).astype(jnp.bfloat16), chosen_rows, 1, 1)
    rank = dot(jnp.where(column < row, 1.0, 0.0).astype(jnp.bfloat16), chosen_rows, 1, 1)
    scores = chosen / (1.0 + jnp.exp(-logits))
    mixing = (scores / jnp.sum(scores, axis=1, keepdims=True)).astype(jnp.bfloat16)
    slot = jnp.where(chosen > 0.0, rank, float(CAP)).astype(jnp.bfloat16)
    packed_ref[:, width:] = jnp.concatenate([slot.astype(jnp.float32), mixing.astype(jnp.float32)], axis=1).astype(jnp.bfloat16)
    places = experts * CAP
    spread = jnp.where(iota((experts, places), 1) // CAP == iota((experts, places), 0), 1.0, 0.0).astype(jnp.bfloat16)
    here = dot(slot, spread) == (iota((tokens, places), 1) % CAP).astype(jnp.float32)
    weights_ref[...] = jnp.where(here, dot(mixing, spread), 0.0).astype(jnp.bfloat16)


def prepare(step, first, arrived, fresh, gain, router, picks):
    tokens, width = arrived.shape
    return pl.pallas_call(
        lambda *refs: prepare_kernel(step, *refs),
        out_shape=(
            jax.ShapeDtypeStruct((tokens, width), jnp.bfloat16),
            jax.ShapeDtypeStruct((tokens, width + LANES), jnp.bfloat16),
            jax.ShapeDtypeStruct((tokens, router.shape[0] * CAP), jnp.bfloat16),
        ),
        in_specs=[SMEM] + [VMEM] * 5,
        out_specs=(VMEM, VMEM, VMEM),
        cost_estimate=BRIEF,
        name="prepare",
    )(first, arrived, fresh, gain, router, picks)


def stacked(pieces):
    return jnp.concatenate([piece.astype(jnp.float32) for piece in pieces], axis=0).astype(jnp.bfloat16)


def dispatch_kernel(block, count, ids_ref, *refs):
    packed_refs, row_refs = refs[:count], refs[count:]
    width = row_refs[0].shape[1]
    rows = row_refs[0].shape[0]
    notes = jnp.concatenate([ref[:, width:] for ref in packed_refs], axis=0)
    tokens = notes.shape[0]
    line, lane = iota((2 * Y * C, LANES), 0), iota((2 * Y * C, LANES), 1)
    select = jnp.zeros((2 * Y * C, LANES), jnp.float32)
    for place in range(Y * C):
        hit = (line == place) & (lane == ids_ref[place])
        select = jnp.where(hit, 1.0, select)
    picked = dot(select.astype(jnp.bfloat16), notes, 1, 1)
    row, token = iota((rows, tokens), 0), iota((rows, tokens), 1)
    code = jnp.where(token // block == row // CAP, row % CAP, -1).astype(jnp.float32)
    picks = []
    for place in range(Y * C):
        here = jnp.broadcast_to(picked[place : place + 1, :], (rows, tokens)) == code
        picks.append(jnp.where(here, 1.0, 0.0))
    pick = jnp.concatenate(picks, axis=0).astype(jnp.bfloat16)

    for cols in column_tiles(width, 512):
        values = jnp.concatenate([ref[:, cols] for ref in packed_refs], axis=0)
        result = dot(pick, values)
        start = 0
        for ref in row_refs:
            ref[:, cols] = result[start : start + ref.shape[0]].astype(jnp.bfloat16)
            start += ref.shape[0]


def dispatch(ids, packed, block):
    width = packed[0].shape[1] - LANES
    tokens = sum(value.shape[0] for value in packed)
    rows = tokens // block * CAP
    return pl.pallas_call(
        lambda *refs: dispatch_kernel(block, len(packed), *refs),
        out_shape=[
            jax.ShapeDtypeStruct((count * rows, width), jnp.bfloat16) for count in (1, C - 1, *[C] * (Y - 1))
        ],
        in_specs=[SMEM] + [VMEM] * len(packed),
        out_specs=[VMEM] * (Y + 1),
        cost_estimate=BRIEF,
        name="dispatch",
    )(ids, *packed)


def travelled(sent):
    own, other = sent[:2]
    there = [along_y(value, step) for step, value in enumerate(sent[2:], 1)]
    return own, other, there


def exchanged(own, other, there):
    half = own.shape[0]
    return [own, *there, to_other_core(jnp.concatenate([other] + [value[half:] for value in there], axis=0))]


def experts_kernel(groups, places_ref, *refs):
    row_refs = [refs[index * (Y + 1) : (index + 1) * (Y + 1)] for index in range(groups)]
    gate_hbm, up_hbm, down_hbm, out_ref = refs[groups * (Y + 1) : groups * (Y + 1) + 4]
    gate_ref, up_ref, down_ref, gated_ref, upper_ref, hidden_ref, arrived = refs[groups * (Y + 1) + 4 :]
    width, inner = gate_ref.shape
    parts, tiles = column_tiles(width, 512), column_tiles(inner, 256)
    copies = []
    for index, part in enumerate(parts):
        for which, (source, target) in enumerate(((gate_hbm, gate_ref), (up_hbm, up_ref))):
            copies.append(pltpu.make_async_copy(source.at[part, :], target.at[part, :], arrived.at[2 * index + which]))
    last = pltpu.make_async_copy(down_hbm, down_ref, arrived.at[2 * len(parts)])
    for copy in copies:
        copy.start()
    last.start()
    gated_ref[...] = jnp.zeros(gated_ref.shape, jnp.float32)
    upper_ref[...] = jnp.zeros(upper_ref.shape, jnp.float32)

    def gather(index, carry):
        part = pl.ds(pl.multiple_of(index * 512, 512), 512)
        pieces = []
        for group in row_refs:
            half = group[0].shape[0]
            pieces += [ref[:half, part] for ref in group[:Y]] + [group[Y][:, part]]
        rows = stacked(pieces)
        for which, (source, target) in enumerate(((gate_hbm, gate_ref), (up_hbm, up_ref))):
            pltpu.make_async_copy(source.at[part, :], target.at[part, :], arrived.at[2 * index + which]).wait()
        for cols in tiles:
            gated_ref[:, cols] += dot(rows, gate_ref[part, cols])
            upper_ref[:, cols] += dot(rows, up_ref[part, cols])
        return carry

    lax.fori_loop(0, len(parts), gather, 0)
    for cols in tiles:
        gate = gated_ref[:, cols]
        hidden_ref[:, cols] = (gate / (1.0 + jnp.exp(-gate)) * upper_ref[:, cols]).astype(jnp.bfloat16)
    last.wait()

    def give(index, carry):
        cols = pl.ds(pl.multiple_of(index * 512, 512), 512)
        result = dot(hidden_ref[...], down_ref[:, cols])
        for place in range(out_ref.shape[0]):
            piece = result[place * CAP : (place + 1) * CAP].astype(jnp.bfloat16)
            out_ref[pl.ds(places_ref[place], 1), :, cols] = piece[None]
        return carry

    lax.fori_loop(0, width // 512, give, 0)


def run_experts(groups, places, w_gate, w_up, w_down):
    width, hidden = w_gate.shape
    operands = []
    for arrays in groups:
        operands += exchanged(*arrays)
    count = places.shape[0] * CAP
    return pl.pallas_call(
        lambda *refs: experts_kernel(len(groups), *refs),
        out_shape=jax.ShapeDtypeStruct((places.shape[0], CAP, width), jnp.bfloat16),
        in_specs=[SMEM] + [VMEM] * len(operands) + [pl.BlockSpec(memory_space=pl.ANY)] * 3,
        out_specs=VMEM,
        scratch_shapes=[
            pltpu.VMEM((width, hidden), jnp.bfloat16),
            pltpu.VMEM((width, hidden), jnp.bfloat16),
            pltpu.VMEM((hidden, width), jnp.bfloat16),
            pltpu.VMEM((count, hidden), jnp.float32),
            pltpu.VMEM((count, hidden), jnp.float32),
            pltpu.VMEM((count, hidden), jnp.bfloat16),
            pltpu.SemaphoreType.DMA((2 * len(column_tiles(width, 512)) + 1,)),
        ],
        compiler_params=pltpu.CompilerParams(vmem_limit_bytes=44 << 20),
        cost_estimate=BRIEF,
        name="experts",
    )(places, *operands, w_gate, w_up, w_down)


def combine_kernel(earlier, current_ref, weights_ref, landed_ref, *refs):
    out_ref = refs[-1]
    weights = weights_ref[...]
    for index in range(earlier):
        out_ref[index] = refs[index][0]
    for cols in column_tiles(out_ref.shape[2], 512):
        total = current_ref[:, cols].astype(jnp.float32) + dot(weights, landed_ref[:, cols])
        out_ref[earlier, :, cols] = total.astype(jnp.bfloat16)


def combine(current, weights, landed, *results):
    return pl.pallas_call(
        lambda *refs: combine_kernel(len(results), *refs),
        out_shape=jax.ShapeDtypeStruct((len(results) + 1, *current.shape), jnp.bfloat16),
        in_specs=[VMEM] * (3 + len(results)),
        out_specs=VMEM,
        cost_estimate=BRIEF,
        name="combine",
    )(current, weights, landed, *results)


NEAR, FAR = (0, -1, 1, -2, 2), (-3, 3, 4)


def section(packed, ids, places, w_gate, w_up, w_down):
    tokens = packed.shape[0]
    part = tokens // 2
    below, above = [packed], [packed]
    for _ in range(2):
        below.append(along_z(below[-1], 1))
        above.append(along_z(above[-1], -1))
    near_rows = dispatch(ids, [packed, below[1], above[1], below[2], above[2]], tokens)
    below.append(along_z(below[2], 1))
    above.append(along_z(above[2], -1))
    third = after(below[3], near_rows[0]), after(above[3], near_rows[0])
    far = [below[3], above[3], along_z(third[0][:part], 1), along_z(third[1][part:], -1)]
    far = far[:2] + [pltpu.with_memory_space_constraint(value, pltpu.VMEM) for value in far[2:]]
    far_rows = dispatch(ids, far, tokens)
    own, other, there = travelled(near_rows)
    near_there = own, other, [after(value, far_rows[0]) for value in there]
    outputs = run_experts([near_there, travelled(far_rows)], places, w_gate, w_up, w_down)
    landed = lax.all_to_all(outputs, GROUP, split_axis=0, concat_axis=0, tiled=True)
    return landed.reshape(-1, landed.shape[-1])


def shards(entering, fresh, w_gate, w_up, w_down, router, gain, routes):
    at_start = (lax.axis_index("segment") == 0).astype(jnp.int32).reshape(1)
    never = jnp.zeros((1,), jnp.int32)
    place, core = lax.axis_index("expert"), lax.axis_index("dp")
    z, y = place // Y, place % Y
    steps = jnp.arange(Y * C, dtype=jnp.int32)
    ids = (z * Y + (y + steps // C) % Y) * C + (core + steps % C) % C
    order = [(block, step, side) for group in (NEAR, FAR) for side in range(C) for step in range(Y) for block in group]
    block, step, side = (jnp.array(column, jnp.int32) for column in zip(*order))
    places = ((z + block + Z) % Z * Y + (y - step + Y) % Y) * C + (core + side) % C
    router_rows = jnp.transpose(router[0])
    picks = jnp.transpose(routes[0], (2, 0, 1))
    w_gate, w_up, w_down = (
        pltpu.with_memory_space_constraint(value[0, 0], pltpu.HBM) for value in (w_gate, w_up, w_down)
    )
    results = []
    count = lax.axis_size("segment")
    for index in range(routes.shape[1]):
        if index == 0:
            first, arrived, other = never, entering[0], entering[0]
        else:
            arrived = lax.ppermute(results[-1][0], "segment", [(i, i + 1) for i in range(count - 1)])
            first, other = at_start, fresh[index - 1]
        current, packed, weights = prepare(index, first, arrived, other, gain, router_rows, picks)
        landed = section(packed, ids, places, w_gate, w_up, w_down)
        results.append(combine(current, weights, landed, *(results if index == routes.shape[1] - 1 else [])))
    return results[-1][None]


def solution(mesh):
    tokens = P("segment", ("expert", "dp"), None)
    weights = P("segment", ("expert", "dp"), None, None)
    in_specs = (
        tokens, P(None, ("expert", "dp"), None), weights, weights, weights,
        P("segment", None, None), P("segment", None), P("segment", None, ("expert", "dp"), None),
    )
    out_specs = P("segment", None, ("expert", "dp"), None)
    return jax.shard_map(shards, mesh=mesh, in_specs=in_specs, out_specs=out_specs, check_vma=False)
```

```python
import jax
import jax.numpy as jnp
from jax import lax
from jax.experimental import pallas as pl
from jax.experimental.pallas import tpu as pltpu
from jax.sharding import PartitionSpec as P

CAP = 8
LANES = 128
GROUP = ("expert", "dp")
Z, Y, C = 8, 4, 2
VMEM = pl.BlockSpec(memory_space=pltpu.VMEM)
BRIEF = pl.CostEstimate(flops=1000, transcendentals=0, bytes_accessed=1000)
SMEM = pl.BlockSpec(memory_space=pltpu.SMEM)


def dot(lhs, rhs, lhs_dim=1, rhs_dim=0):
    return lax.dot_general(
        lhs, rhs, (((lhs_dim,), (rhs_dim,)), ((), ())), preferred_element_type=jnp.float32
    )


def column_tiles(width, tile):
    return [slice(start, min(start + tile, width)) for start in range(0, width, tile)]


def iota(shape, dim):
    return lax.broadcasted_iota(jnp.int32, shape, dim)


def move(value, target):
    pairs = []
    for z in range(Z):
        for y in range(Y):
            for core in range(C):
                to_z, to_y, to_core = target(z, y, core)
                pairs.append(((z * Y + y) * C + core, ((to_z % Z) * Y + to_y % Y) * C + to_core))
    return lax.ppermute(value, GROUP, pairs)


def to_other_core(value):
    return move(value, lambda z, y, core: (z, y, 1 - core))


def along_y(value, steps):
    return value if steps == 0 else move(value, lambda z, y, core: (z, y + steps, core))


def along_z(value, steps):
    return move(value, lambda z, y, core: (z + steps, y, core))


def held_close(value):
    return pltpu.with_memory_space_constraint(value, pltpu.VMEM)


def after(value, *others):
    return lax.optimization_barrier((value, *others))[0]


def prepare_kernel(step, first_ref, arrived_ref, fresh_ref, gain_ref, router_ref, picks_ref,
                   current_ref, packed_ref, weights_ref):
    tokens, width = current_ref.shape
    experts = router_ref.shape[0]
    current = jnp.where(first_ref[0] == 1, fresh_ref[...], arrived_ref[...])
    current_ref[...] = current
    values = current.astype(jnp.float32)
    inv_scale = lax.rsqrt(jnp.mean(values * values, axis=1, keepdims=True) + 1e-06)
    normed = (values * inv_scale * gain_ref[...]).astype(jnp.bfloat16)
    packed_ref[:, :width] = normed
    logits = dot(normed, router_ref[...], 1, 1)
    expert_ids = iota((experts, tokens), 0)
    chosen_rows = jnp.zeros((experts, tokens), jnp.float32)
    for choice in range(picks_ref.shape[0]):
        chosen_rows += jnp.where(picks_ref[choice, step : step + 1, :] == expert_ids, 1.0, 0.0)
    chosen_rows = chosen_rows.astype(jnp.bfloat16)
    row, column = iota((tokens, tokens), 0), iota((tokens, tokens), 1)
    chosen = dot(jnp.where(row == column, 1.0, 0.0).astype(jnp.bfloat16), chosen_rows, 1, 1)
    rank = dot(jnp.where(column < row, 1.0, 0.0).astype(jnp.bfloat16), chosen_rows, 1, 1)
    scores = chosen / (1.0 + jnp.exp(-logits))
    mixing = (scores / jnp.sum(scores, axis=1, keepdims=True)).astype(jnp.bfloat16)
    slot = jnp.where(chosen > 0.0, rank, float(CAP)).astype(jnp.bfloat16)
    packed_ref[:, width:] = jnp.concatenate([slot.astype(jnp.float32), mixing.astype(jnp.float32)], axis=1).astype(jnp.bfloat16)
    places = experts * CAP
    spread = jnp.where(iota((experts, places), 1) // CAP == iota((experts, places), 0), 1.0, 0.0).astype(jnp.bfloat16)
    here = dot(slot, spread) == (iota((tokens, places), 1) % CAP).astype(jnp.float32)
    weights_ref[...] = jnp.where(here, dot(mixing, spread), 0.0).astype(jnp.bfloat16)


def prepare(step, first, arrived, fresh, gain, router, picks):
    tokens, width = arrived.shape
    return pl.pallas_call(
        lambda *refs: prepare_kernel(step, *refs),
        out_shape=(
            jax.ShapeDtypeStruct((tokens, width), jnp.bfloat16),
            jax.ShapeDtypeStruct((tokens, width + LANES), jnp.bfloat16),
            jax.ShapeDtypeStruct((tokens, router.shape[0] * CAP), jnp.bfloat16),
        ),
        in_specs=[SMEM] + [VMEM] * 5,
        out_specs=(VMEM, VMEM, VMEM),
        cost_estimate=BRIEF,
        name="prepare",
    )(first, arrived, fresh, gain, router, picks)


def stacked(pieces):
    return jnp.concatenate([piece.astype(jnp.float32) for piece in pieces], axis=0).astype(jnp.bfloat16)


def dispatch_kernel(block, count, ids_ref, *refs):
    packed_refs, row_refs = refs[:count], refs[count:]
    width = row_refs[0].shape[1]
    rows = row_refs[0].shape[0]
    notes = jnp.concatenate([ref[:, width:] for ref in packed_refs], axis=0)
    tokens = notes.shape[0]
    line, lane = iota((2 * Y * C, LANES), 0), iota((2 * Y * C, LANES), 1)
    select = jnp.zeros((2 * Y * C, LANES), jnp.float32)
    for place in range(Y * C):
        hit = (line == place) & (lane == ids_ref[place])
        select = jnp.where(hit, 1.0, select)
    picked = dot(select.astype(jnp.bfloat16), notes, 1, 1)
    row, token = iota((rows, tokens), 0), iota((rows, tokens), 1)
    code = jnp.where(token // block == row // CAP, row % CAP, -1).astype(jnp.float32)
    picks = []
    for place in range(Y * C):
        here = jnp.broadcast_to(picked[place : place + 1, :], (rows, tokens)) == code
        picks.append(jnp.where(here, 1.0, 0.0))
    pick = jnp.concatenate(picks, axis=0).astype(jnp.bfloat16)

    for cols in column_tiles(width, 512):
        values = jnp.concatenate([ref[:, cols] for ref in packed_refs], axis=0)
        result = dot(pick, values)
        start = 0
        for ref in row_refs:
            ref[:, cols] = result[start : start + ref.shape[0]].astype(jnp.bfloat16)
            start += ref.shape[0]


def dispatch(ids, packed, block):
    width = packed[0].shape[1] - LANES
    tokens = sum(value.shape[0] for value in packed)
    rows = tokens // block * CAP
    return pl.pallas_call(
        lambda *refs: dispatch_kernel(block, len(packed), *refs),
        out_shape=[
            jax.ShapeDtypeStruct((count * rows, width), jnp.bfloat16) for count in (1, C - 1, *[C] * (Y - 1))
        ],
        in_specs=[SMEM] + [VMEM] * len(packed),
        out_specs=[VMEM] * (Y + 1),
        cost_estimate=BRIEF,
        name="dispatch",
    )(ids, *packed)


def travelled(sent):
    own, other = sent[:2]
    there = [along_y(value, step) for step, value in enumerate(sent[2:], 1)]
    return own, other, there


def exchanged(own, other, there):
    half = own.shape[0]
    return [own, *there, to_other_core(jnp.concatenate([other] + [value[half:] for value in there], axis=0))]


def experts_kernel(groups, places_ref, *refs):
    row_refs = [refs[index * (Y + 1) : (index + 1) * (Y + 1)] for index in range(groups)]
    gate_hbm, up_hbm, down_hbm, out_ref = refs[groups * (Y + 1) : groups * (Y + 1) + 4]
    gate_ref, up_ref, down_ref, gated_ref, upper_ref, hidden_ref, arrived = refs[groups * (Y + 1) + 4 :]
    width, inner = gate_ref.shape
    parts, tiles = column_tiles(width, 512), column_tiles(inner, 256)
    copies = []
    for index, part in enumerate(parts):
        for which, (source, target) in enumerate(((gate_hbm, gate_ref), (up_hbm, up_ref))):
            copies.append(pltpu.make_async_copy(source.at[part, :], target.at[part, :], arrived.at[2 * index + which]))
    last = pltpu.make_async_copy(down_hbm, down_ref, arrived.at[2 * len(parts)])
    for copy in copies:
        copy.start()
    last.start()
    gated_ref[...] = jnp.zeros(gated_ref.shape, jnp.float32)
    upper_ref[...] = jnp.zeros(upper_ref.shape, jnp.float32)

    def gather(index, carry):
        part = pl.ds(pl.multiple_of(index * 512, 512), 512)
        pieces = []
        for group in row_refs:
            half = group[0].shape[0]
            pieces += [ref[:half, part] for ref in group[:Y]] + [group[Y][:, part]]
        rows = stacked(pieces)
        for which, (source, target) in enumerate(((gate_hbm, gate_ref), (up_hbm, up_ref))):
            pltpu.make_async_copy(source.at[part, :], target.at[part, :], arrived.at[2 * index + which]).wait()
        for cols in tiles:
            gated_ref[:, cols] += dot(rows, gate_ref[part, cols])
            upper_ref[:, cols] += dot(rows, up_ref[part, cols])
        return carry

    lax.fori_loop(0, len(parts), gather, 0)
    for cols in tiles:
        gate = gated_ref[:, cols]
        hidden_ref[:, cols] = (gate / (1.0 + jnp.exp(-gate)) * upper_ref[:, cols]).astype(jnp.bfloat16)
    last.wait()

    hidden = hidden_ref[...]
    for cols in column_tiles(width, 512):
        result = dot(hidden, down_ref[:, cols])
        for place in range(out_ref.shape[0]):
            piece = result[place * CAP : (place + 1) * CAP].astype(jnp.bfloat16)
            out_ref[pl.ds(places_ref[place], 1), :, cols] = piece[None]


def run_experts(groups, places, w_gate, w_up, w_down):
    width, hidden = w_gate.shape
    operands = []
    for arrays in groups:
        operands += exchanged(*arrays)
    count = places.shape[0] * CAP
    return pl.pallas_call(
        lambda *refs: experts_kernel(len(groups), *refs),
        out_shape=jax.ShapeDtypeStruct((places.shape[0], CAP, width), jnp.bfloat16),
        in_specs=[SMEM] + [VMEM] * len(operands) + [pl.BlockSpec(memory_space=pl.ANY)] * 3,
        out_specs=VMEM,
        scratch_shapes=[
            pltpu.VMEM((width, hidden), jnp.bfloat16),
            pltpu.VMEM((width, hidden), jnp.bfloat16),
            pltpu.VMEM((hidden, width), jnp.bfloat16),
            pltpu.VMEM((count, hidden), jnp.float32),
            pltpu.VMEM((count, hidden), jnp.float32),
            pltpu.VMEM((count, hidden), jnp.bfloat16),
            pltpu.SemaphoreType.DMA((2 * len(column_tiles(width, 512)) + 1,)),
        ],
        compiler_params=pltpu.CompilerParams(vmem_limit_bytes=44 << 20),
        cost_estimate=BRIEF,
        name="experts",
    )(places, *operands, w_gate, w_up, w_down)


def combine_kernel(earlier, current_ref, weights_ref, landed_ref, *refs):
    out_ref = refs[-1]
    weights = weights_ref[...]
    for index in range(earlier):
        out_ref[index] = refs[index][0]
    for cols in column_tiles(out_ref.shape[2], 512):
        total = current_ref[:, cols].astype(jnp.float32) + dot(weights, landed_ref[:, cols])
        out_ref[earlier, :, cols] = total.astype(jnp.bfloat16)


def combine(current, weights, landed, *results):
    return pl.pallas_call(
        lambda *refs: combine_kernel(len(results), *refs),
        out_shape=jax.ShapeDtypeStruct((len(results) + 1, *current.shape), jnp.bfloat16),
        in_specs=[VMEM] * (3 + len(results)),
        out_specs=VMEM,
        cost_estimate=BRIEF,
        name="combine",
    )(current, weights, landed, *results)


NEAR, FAR = (0, -1, 1, -2, 2), (-3, 3, 4)


def section(packed, ids, places, w_gate, w_up, w_down):
    tokens = packed.shape[0]
    part = tokens // 2
    below, above = [packed], [packed]
    for _ in range(2):
        below.append(along_z(below[-1], 1))
        above.append(along_z(above[-1], -1))
    near = [packed] + [held_close(value) for value in (below[1], above[1], below[2], above[2])]
    near_rows = dispatch(ids, near, tokens)
    below.append(along_z(below[2], 1))
    above.append(along_z(above[2], -1))
    third = after(below[3], near_rows[0]), after(above[3], near_rows[0])
    far = [below[3], above[3], along_z(third[0][:part], 1), along_z(third[1][part:], -1)]
    far_rows = dispatch(ids, [held_close(value) for value in far], tokens)
    own, other, there = travelled(near_rows)
    near_there = own, other, [after(value, far_rows[0]) for value in there]
    outputs = run_experts([near_there, travelled(far_rows)], places, w_gate, w_up, w_down)
    landed = lax.all_to_all(outputs, GROUP, split_axis=0, concat_axis=0, tiled=True)
    return held_close(landed.reshape(-1, landed.shape[-1]))


def shards(entering, fresh, w_gate, w_up, w_down, router, gain, routes):
    at_start = (lax.axis_index("segment") == 0).astype(jnp.int32).reshape(1)
    never = jnp.zeros((1,), jnp.int32)
    place, core = lax.axis_index("expert"), lax.axis_index("dp")
    z, y = place // Y, place % Y
    steps = jnp.arange(Y * C, dtype=jnp.int32)
    ids = (z * Y + (y + steps // C) % Y) * C + (core + steps % C) % C
    order = [(block, step, side) for group in (NEAR, FAR) for side in range(C) for step in range(Y) for block in group]
    block, step, side = (jnp.array(column, jnp.int32) for column in zip(*order))
    places = ((z + block + Z) % Z * Y + (y - step + Y) % Y) * C + (core + side) % C
    router_rows = jnp.transpose(router[0])
    picks = jnp.transpose(routes[0], (2, 0, 1))
    w_gate, w_up, w_down = (
        pltpu.with_memory_space_constraint(value[0, 0], pltpu.HBM) for value in (w_gate, w_up, w_down)
    )
    results = []
    count = lax.axis_size("segment")
    for index in range(routes.shape[1]):
        if index == 0:
            first, arrived, other = never, entering[0], entering[0]
        else:
            arrived = held_close(lax.ppermute(results[-1][0], "segment", [(i, i + 1) for i in range(count - 1)]))
            first, other = at_start, fresh[index - 1]
        current, packed, weights = prepare(index, first, arrived, other, gain, router_rows, picks)
        landed = section(packed, ids, places, w_gate, w_up, w_down)
        results.append(combine(current, weights, landed, *(results if index == routes.shape[1] - 1 else [])))
    return results[-1][None]


def solution(mesh):
    tokens = P("segment", ("expert", "dp"), None)
    weights = P("segment", ("expert", "dp"), None, None)
    in_specs = (
        tokens, P(None, ("expert", "dp"), None), weights, weights, weights,
        P("segment", None, None), P("segment", None), P("segment", None, ("expert", "dp"), None),
    )
    out_specs = P("segment", None, ("expert", "dp"), None)
    return jax.shard_map(shards, mesh=mesh, in_specs=in_specs, out_specs=out_specs, check_vma=False)
```

```python
import jax
import jax.numpy as jnp
from jax import lax
from jax.experimental import pallas as pl
from jax.experimental.pallas import tpu as pltpu
from jax.sharding import PartitionSpec as P

CAP = 8
LANES = 128
GROUP = ("expert", "dp")
Z, Y, C = 8, 4, 2
VMEM = pl.BlockSpec(memory_space=pltpu.VMEM)
BRIEF = pl.CostEstimate(flops=1000, transcendentals=0, bytes_accessed=1000)
SMEM = pl.BlockSpec(memory_space=pltpu.SMEM)


def dot(lhs, rhs, lhs_dim=1, rhs_dim=0):
    return lax.dot_general(
        lhs, rhs, (((lhs_dim,), (rhs_dim,)), ((), ())), preferred_element_type=jnp.float32
    )


def column_tiles(width, tile):
    return [slice(start, min(start + tile, width)) for start in range(0, width, tile)]


def iota(shape, dim):
    return lax.broadcasted_iota(jnp.int32, shape, dim)


def move(value, target):
    pairs = []
    for z in range(Z):
        for y in range(Y):
            for core in range(C):
                to_z, to_y, to_core = target(z, y, core)
                pairs.append(((z * Y + y) * C + core, ((to_z % Z) * Y + to_y % Y) * C + to_core))
    return lax.ppermute(value, GROUP, pairs)


def to_other_core(value):
    return move(value, lambda z, y, core: (z, y, 1 - core))


def along_y(value, steps):
    return value if steps == 0 else move(value, lambda z, y, core: (z, y + steps, core))


def along_z(value, steps):
    return move(value, lambda z, y, core: (z + steps, y, core))


def held_close(value):
    return pltpu.with_memory_space_constraint(value, pltpu.VMEM)


def after(value, *others):
    return lax.optimization_barrier((value, *others))[0]


def prepare_kernel(step, first_ref, arrived_ref, fresh_ref, gain_ref, router_ref, picks_ref,
                   current_ref, packed_ref, weights_ref):
    tokens, width = current_ref.shape
    experts = router_ref.shape[0]
    current = jnp.where(first_ref[0] == 1, fresh_ref[...], arrived_ref[...])
    current_ref[...] = current
    values = current.astype(jnp.float32)
    inv_scale = lax.rsqrt(jnp.mean(values * values, axis=1, keepdims=True) + 1e-06)
    normed = (values * inv_scale * gain_ref[...]).astype(jnp.bfloat16)
    packed_ref[:, :width] = normed
    logits = dot(normed, router_ref[...], 1, 1)
    expert_ids = iota((experts, tokens), 0)
    chosen_rows = jnp.zeros((experts, tokens), jnp.float32)
    for choice in range(picks_ref.shape[0]):
        chosen_rows += jnp.where(picks_ref[choice, step : step + 1, :] == expert_ids, 1.0, 0.0)
    chosen_rows = chosen_rows.astype(jnp.bfloat16)
    row, column = iota((tokens, tokens), 0), iota((tokens, tokens), 1)
    chosen = dot(jnp.where(row == column, 1.0, 0.0).astype(jnp.bfloat16), chosen_rows, 1, 1)
    rank = dot(jnp.where(column < row, 1.0, 0.0).astype(jnp.bfloat16), chosen_rows, 1, 1)
    scores = chosen / (1.0 + jnp.exp(-logits))
    mixing = (scores / jnp.sum(scores, axis=1, keepdims=True)).astype(jnp.bfloat16)
    slot = jnp.where(chosen > 0.0, rank, float(CAP)).astype(jnp.bfloat16)
    packed_ref[:, width:] = jnp.concatenate([slot.astype(jnp.float32), mixing.astype(jnp.float32)], axis=1).astype(jnp.bfloat16)
    places = experts * CAP
    spread = jnp.where(iota((experts, places), 1) // CAP == iota((experts, places), 0), 1.0, 0.0).astype(jnp.bfloat16)
    here = dot(slot, spread) == (iota((tokens, places), 1) % CAP).astype(jnp.float32)
    weights_ref[...] = jnp.where(here, dot(mixing, spread), 0.0).astype(jnp.bfloat16)


def prepare(step, first, arrived, fresh, gain, router, picks):
    tokens, width = arrived.shape
    return pl.pallas_call(
        lambda *refs: prepare_kernel(step, *refs),
        out_shape=(
            jax.ShapeDtypeStruct((tokens, width), jnp.bfloat16),
            jax.ShapeDtypeStruct((tokens, width + LANES), jnp.bfloat16),
            jax.ShapeDtypeStruct((tokens, router.shape[0] * CAP), jnp.bfloat16),
        ),
        in_specs=[SMEM] + [VMEM] * 5,
        out_specs=(VMEM, VMEM, VMEM),
        cost_estimate=BRIEF,
        name="prepare",
    )(first, arrived, fresh, gain, router, picks)


def stacked(pieces):
    return jnp.concatenate([piece.astype(jnp.float32) for piece in pieces], axis=0).astype(jnp.bfloat16)


def dispatch_kernel(block, count, ids_ref, *refs):
    packed_refs, row_refs = refs[:count], refs[count:]
    width = row_refs[0].shape[1]
    rows = row_refs[0].shape[0]
    notes = jnp.concatenate([ref[:, width:] for ref in packed_refs], axis=0)
    tokens = notes.shape[0]
    line, lane = iota((2 * Y * C, LANES), 0), iota((2 * Y * C, LANES), 1)
    select = jnp.zeros((2 * Y * C, LANES), jnp.float32)
    for place in range(Y * C):
        hit = (line == place) & (lane == ids_ref[place])
        select = jnp.where(hit, 1.0, select)
    picked = dot(select.astype(jnp.bfloat16), notes, 1, 1)
    row, token = iota((rows, tokens), 0), iota((rows, tokens), 1)
    code = jnp.where(token // block == row // CAP, row % CAP, -1).astype(jnp.float32)
    picks = []
    for place in range(Y * C):
        here = jnp.broadcast_to(picked[place : place + 1, :], (rows, tokens)) == code
        picks.append(jnp.where(here, 1.0, 0.0))
    pick = jnp.concatenate(picks, axis=0).astype(jnp.bfloat16)

    for cols in column_tiles(width, 512):
        values = jnp.concatenate([ref[:, cols] for ref in packed_refs], axis=0)
        result = dot(pick, values)
        start = 0
        for ref in row_refs:
            ref[:, cols] = result[start : start + ref.shape[0]].astype(jnp.bfloat16)
            start += ref.shape[0]


def dispatch(ids, packed, block):
    width = packed[0].shape[1] - LANES
    tokens = sum(value.shape[0] for value in packed)
    rows = tokens // block * CAP
    return pl.pallas_call(
        lambda *refs: dispatch_kernel(block, len(packed), *refs),
        out_shape=[
            jax.ShapeDtypeStruct((count * rows, width), jnp.bfloat16) for count in (1, C - 1, *[C] * (Y - 1))
        ],
        in_specs=[SMEM] + [VMEM] * len(packed),
        out_specs=[VMEM] * (Y + 1),
        cost_estimate=BRIEF,
        name="dispatch",
    )(ids, *packed)


def travelled(sent):
    own, other = sent[:2]
    there = [along_y(value, step) for step, value in enumerate(sent[2:], 1)]
    return own, other, there


def exchanged(own, other, there):
    half = own.shape[0]
    return [own, *there, to_other_core(jnp.concatenate([other] + [value[half:] for value in there], axis=0))]


def experts_kernel(groups, places_ref, *refs):
    row_refs = [refs[index * (Y + 1) : (index + 1) * (Y + 1)] for index in range(groups)]
    gate_hbm, up_hbm, down_hbm, out_ref = refs[groups * (Y + 1) : groups * (Y + 1) + 4]
    gate_ref, up_ref, down_ref, gated_ref, upper_ref, hidden_ref, arrived = refs[groups * (Y + 1) + 4 :]
    width, inner = gate_ref.shape
    parts, tiles = column_tiles(width, 512), column_tiles(inner, 256)
    copies = []
    for index, part in enumerate(parts):
        for which, (source, target) in enumerate(((gate_hbm, gate_ref), (up_hbm, up_ref))):
            copies.append(pltpu.make_async_copy(source.at[part, :], target.at[part, :], arrived.at[2 * index + which]))
    last = pltpu.make_async_copy(down_hbm, down_ref, arrived.at[2 * len(parts)])
    for copy in copies:
        copy.start()
    last.start()
    gated_ref[...] = jnp.zeros(gated_ref.shape, jnp.float32)
    upper_ref[...] = jnp.zeros(upper_ref.shape, jnp.float32)

    def gather(index, carry):
        part = pl.ds(pl.multiple_of(index * 512, 512), 512)
        pieces = []
        for group in row_refs:
            half = group[0].shape[0]
            pieces += [ref[:half, part] for ref in group[:Y]] + [group[Y][:, part]]
        rows = stacked(pieces)
        for which, (source, target) in enumerate(((gate_hbm, gate_ref), (up_hbm, up_ref))):
            pltpu.make_async_copy(source.at[part, :], target.at[part, :], arrived.at[2 * index + which]).wait()
        for cols in tiles:
            gated_ref[:, cols] += dot(rows, gate_ref[part, cols])
            upper_ref[:, cols] += dot(rows, up_ref[part, cols])
        return carry

    lax.fori_loop(0, len(parts), gather, 0)
    for cols in tiles:
        gate = gated_ref[:, cols]
        hidden_ref[:, cols] = (gate / (1.0 + jnp.exp(-gate)) * upper_ref[:, cols]).astype(jnp.bfloat16)
    last.wait()

    hidden = hidden_ref[...]
    for cols in column_tiles(width, 512):
        result = dot(hidden, down_ref[:, cols])
        for place in range(out_ref.shape[0]):
            piece = result[place * CAP : (place + 1) * CAP].astype(jnp.bfloat16)
            out_ref[pl.ds(places_ref[place], 1), :, cols] = piece[None]


def run_experts(groups, places, w_gate, w_up, w_down):
    width, hidden = w_gate.shape
    operands = []
    for arrays in groups:
        operands += exchanged(*arrays)
    count = places.shape[0] * CAP
    return pl.pallas_call(
        lambda *refs: experts_kernel(len(groups), *refs),
        out_shape=jax.ShapeDtypeStruct((places.shape[0], CAP, width), jnp.bfloat16),
        in_specs=[SMEM] + [VMEM] * len(operands) + [pl.BlockSpec(memory_space=pl.ANY)] * 3,
        out_specs=VMEM,
        scratch_shapes=[
            pltpu.VMEM((width, hidden), jnp.bfloat16),
            pltpu.VMEM((width, hidden), jnp.bfloat16),
            pltpu.VMEM((hidden, width), jnp.bfloat16),
            pltpu.VMEM((count, hidden), jnp.float32),
            pltpu.VMEM((count, hidden), jnp.float32),
            pltpu.VMEM((count, hidden), jnp.bfloat16),
            pltpu.SemaphoreType.DMA((2 * len(column_tiles(width, 512)) + 1,)),
        ],
        compiler_params=pltpu.CompilerParams(vmem_limit_bytes=44 << 20),
        cost_estimate=BRIEF,
        name="experts",
    )(places, *operands, w_gate, w_up, w_down)


def combine_kernel(earlier, current_ref, weights_ref, landed_ref, *refs):
    out_ref = refs[-1]
    weights = weights_ref[...]
    for index in range(earlier):
        out_ref[index] = refs[index][0]
    for cols in column_tiles(out_ref.shape[2], 512):
        total = current_ref[:, cols].astype(jnp.float32) + dot(weights, landed_ref[:, cols])
        out_ref[earlier, :, cols] = total.astype(jnp.bfloat16)


def combine(current, weights, landed, *results):
    return pl.pallas_call(
        lambda *refs: combine_kernel(len(results), *refs),
        out_shape=jax.ShapeDtypeStruct((len(results) + 1, *current.shape), jnp.bfloat16),
        in_specs=[VMEM] * (3 + len(results)),
        out_specs=VMEM,
        cost_estimate=BRIEF,
        name="combine",
    )(current, weights, landed, *results)


NEAR, FAR = (0, -1, 1, -2, 2), (-3, 3, 4)


def section(packed, ids, places, w_gate, w_up, w_down):
    tokens = packed.shape[0]
    part = tokens // 2
    below, above = [packed], [packed]
    for hop in range(2):
        below.append(along_z(after(below[-1], ids, places) if hop else below[-1], 1))
        above.append(along_z(above[-1], -1))
    near = [packed] + [held_close(value) for value in (below[1], above[1], below[2], above[2])]
    near_rows = dispatch(ids, near, tokens)
    below.append(along_z(below[2], 1))
    above.append(along_z(above[2], -1))
    third = after(below[3], near_rows[0]), after(above[3], near_rows[0])
    far = [below[3], above[3], along_z(third[0][:part], 1), along_z(third[1][part:], -1)]
    far_rows = dispatch(ids, [held_close(value) for value in far], tokens)
    own, other, there = travelled(near_rows)
    near_there = own, other, [after(value, far_rows[0]) for value in there]
    outputs = run_experts([near_there, travelled(far_rows)], places, w_gate, w_up, w_down)
    landed = lax.all_to_all(outputs, GROUP, split_axis=0, concat_axis=0, tiled=True)
    return held_close(landed.reshape(-1, landed.shape[-1]))


def shards(entering, fresh, w_gate, w_up, w_down, router, gain, routes):
    at_start = (lax.axis_index("segment") == 0).astype(jnp.int32).reshape(1)
    never = jnp.zeros((1,), jnp.int32)
    place, core = lax.axis_index("expert"), lax.axis_index("dp")
    z, y = place // Y, place % Y
    steps = jnp.arange(Y * C, dtype=jnp.int32)
    ids = (z * Y + (y + steps // C) % Y) * C + (core + steps % C) % C
    order = [(block, step, side) for group in (NEAR, FAR) for side in range(C) for step in range(Y) for block in group]
    block, step, side = (jnp.array(column, jnp.int32) for column in zip(*order))
    places = ((z + block + Z) % Z * Y + (y - step + Y) % Y) * C + (core + side) % C
    router_rows = jnp.transpose(router[0])
    picks = jnp.transpose(routes[0], (2, 0, 1))
    w_gate, w_up, w_down = (
        pltpu.with_memory_space_constraint(value[0, 0], pltpu.HBM) for value in (w_gate, w_up, w_down)
    )
    results = []
    count = lax.axis_size("segment")
    for index in range(routes.shape[1]):
        if index == 0:
            first, arrived, other = never, entering[0], entering[0]
        else:
            arrived = held_close(lax.ppermute(results[-1][0], "segment", [(i, i + 1) for i in range(count - 1)]))
            first, other = at_start, fresh[index - 1]
        current, packed, weights = prepare(index, first, arrived, other, gain, router_rows, picks)
        landed = section(packed, ids, places, w_gate, w_up, w_down)
        results.append(combine(current, weights, landed, *(results if index == routes.shape[1] - 1 else [])))
    return results[-1][None]


def solution(mesh):
    tokens = P("segment", ("expert", "dp"), None)
    weights = P("segment", ("expert", "dp"), None, None)
    in_specs = (
        tokens, P(None, ("expert", "dp"), None), weights, weights, weights,
        P("segment", None, None), P("segment", None), P("segment", None, ("expert", "dp"), None),
    )
    out_specs = P("segment", None, ("expert", "dp"), None)
    return jax.shard_map(shards, mesh=mesh, in_specs=in_specs, out_specs=out_specs, check_vma=False)
```
